256 devices in a mesh: blk: 32 (over y_lo, z, core), uly: 8 (over y_hi, x).
Axes of the slice: x: 4, y: 4 (y_hi: 2, y_lo: 2; y = y_hi * 2 + y_lo), z: 8, core: 2. Of those that a mesh axis runs over, the one named last changes fastest.
Arguments:
- tokens: bfloat16 [32768, 5120], P(('blk', 'uly')), may hold values from -6 to 6
- query_base: bfloat16 [32768, 5120], P(('blk', 'uly')), may hold values from -9 to 9
- key_base: bfloat16 [32768, 5120], P(('blk', 'uly')), may hold values from -9 to 9
- value_base: bfloat16 [32768, 5120], P(('blk', 'uly')), may hold values from -6 to 6
- out_grad: bfloat16 [32768, 5120], P(('blk', 'uly')), may hold values from -0.059814453 to 0.059814453
- down_q: bfloat16 [5120, 64], replicated, may hold values from -0.078125 to 0.078125
- up_q: bfloat16 [64, 5120], replicated, may hold values from -0.75 to 0.75
- down_v: bfloat16 [5120, 64], replicated, may hold values from -0.078125 to 0.078125
- up_v: bfloat16 [64, 5120], replicated, may hold values from -0.75 to 0.75
Outputs:
- attended: bfloat16 [32768, 5120], P(('blk', 'uly'))
- grad_down_q: bfloat16 [5120, 64], replicated
- grad_up_q: bfloat16 [64, 5120], P(None, 'uly')
- grad_down_v: bfloat16 [5120, 64], replicated
- grad_up_v: bfloat16 [64, 5120], P(None, 'uly')
The draws below stay inside these ranges and needn't reach their ends.
All inputs are finite; a program needn't handle non-finite values.
Results may differ from the reference program's by a relative error of at most 0.025.
Values may be sent and summed in bfloat16 or wider, within the bound.
No kernel may reach another device: no remote copies, remote signals or barrier semaphores. Data moves between devices by JAX's collectives and lax.ppermute only.
A program may use at most 128 MiB of HBM per device.

```python
import jax
import jax.numpy as jnp
from jax import lax

D = 5120
HEADS = 40
HEAD = 128
RANK = 64
BLOCK = 1024
TOKENS = 32768


def shared_bases(key):
    base = jax.random.fold_in(key, 7)
    key_query, key_keys = jax.random.split(base, 2)
    query = jnp.clip(1.5 * jax.random.normal(key_query, (TOKENS, D), jnp.float32), -9.0, 9.0)
    keys = jnp.clip(1.5 * jax.random.normal(key_keys, (TOKENS, D), jnp.float32), -9.0, 9.0)
    return (query, keys)


def draw_query_base(key, part):
    return shared_bases(key)[0].astype(jnp.bfloat16)


def draw_key_base(key, part):
    return shared_bases(key)[1].astype(jnp.bfloat16)


def shard_levels(rng, dims, shards, low, top_value):
    gain = 1.0
    for axis_at, blocks in shards:
        steps = jax.random.uniform(jax.random.fold_in(jax.random.fold_in(rng, 6), axis_at), (blocks,), jnp.float32, low / len(shards), top_value / len(shards))
        gain = gain * jnp.repeat(jnp.exp(steps), dims[axis_at] // blocks).reshape((-1,) + (1,) * (len(dims) - 1 - axis_at))
    return gain


def scatter_about(own_key, dims, deviation, bound, cuts=(), held_as=jnp.bfloat16):
    result = jax.random.normal(own_key, dims, jnp.float32) * deviation
    if len(cuts) > 0:
        result = shard_levels(own_key, dims, cuts, -0.22, 0.18) * result
    return jnp.clip(result, min=-bound, max=bound).astype(held_as)


def setup_inputs(seed: int = 0) -> dict:
    key_of = jax.random.split(jax.random.key(seed), 10)
    tokens = scatter_about(key_of[0], (TOKENS, D), 1.0, 6.0, ((0, 256),))
    query_base = draw_query_base(jax.random.fold_in(key_of[9], 71), 0)
    key_base = draw_key_base(jax.random.fold_in(key_of[9], 71), 0)
    value_base = scatter_about(key_of[3], (TOKENS, D), 1.0, 6.0, ((0, 256),))
    out_grad = scatter_about(key_of[4], (TOKENS, D), 0.01, 0.059814453, ((0, 256),))
    down_q = scatter_about(key_of[5], (D, RANK), D ** -0.5, 0.078125)
    up_q = scatter_about(key_of[6], (RANK, D), RANK ** -0.5, 0.75)
    down_v = scatter_about(key_of[7], (D, RANK), D ** -0.5, 0.078125)
    up_v = scatter_about(key_of[8], (RANK, D), RANK ** -0.5, 0.75)
    return {"tokens": tokens, "query_base": query_base, "key_base": key_base, "value_base": value_base, "out_grad": out_grad, "down_q": down_q, "up_q": up_q, "down_v": down_v, "up_v": up_v}


def inner(left, right):
    return lax.dot_general(left, right, (((0,), (0,)), ((), ())), preferred_element_type=jnp.float32)


def head_pass(query, keys, values, upstream, usable, scale):
    scores = jnp.dot(query, keys.T, preferred_element_type=jnp.float32) * scale
    scores = jnp.where(usable[None, :], scores, -jnp.inf)
    top = jnp.max(scores, axis=1, keepdims=True)
    total = jnp.sum(jnp.exp(scores - top), axis=1, keepdims=True)
    probs = jnp.exp(scores - top - jnp.log(total)).astype(jnp.bfloat16)
    attended = jnp.dot(probs, values, preferred_element_type=jnp.float32).astype(jnp.bfloat16)
    delta = jnp.sum(upstream.astype(jnp.float32) * attended.astype(jnp.float32), axis=1, keepdims=True)
    prob_grad = jnp.dot(upstream, values.T, preferred_element_type=jnp.float32)
    score_grad = (probs.astype(jnp.float32) * (prob_grad - delta)).astype(jnp.bfloat16)
    query_grad = (jnp.dot(score_grad, keys, preferred_element_type=jnp.float32) * scale).astype(jnp.bfloat16)
    value_terms = jnp.dot(probs.T, upstream, preferred_element_type=jnp.float32)
    return attended, query_grad, value_terms


def reference(tokens, query_base, key_base, value_base, out_grad, down_q, up_q, down_v, up_v):
    low_q = jnp.dot(tokens, down_q, preferred_element_type=jnp.float32).astype(jnp.bfloat16)
    low_v = jnp.dot(tokens, down_v, preferred_element_type=jnp.float32).astype(jnp.bfloat16)
    query = (query_base.astype(jnp.float32) + jnp.dot(low_q, up_q, preferred_element_type=jnp.float32)).astype(jnp.bfloat16)
    value = (value_base.astype(jnp.float32) + jnp.dot(low_v, up_v, preferred_element_type=jnp.float32)).astype(jnp.bfloat16)
    nblocks = TOKENS // BLOCK

    def blocks(array):
        return array.reshape(nblocks, BLOCK, HEADS, HEAD).transpose(0, 2, 1, 3)

    query_b = blocks(query)
    keys_b = blocks(key_base)
    values_b = blocks(value)
    upstream_b = blocks(out_grad)
    keys_p = jnp.concatenate([jnp.zeros_like(keys_b[:1]), keys_b[:-1]], 0)
    values_p = jnp.concatenate([jnp.zeros_like(values_b[:1]), values_b[:-1]], 0)
    column = jnp.arange(2 * BLOCK)
    scale = HEAD ** -0.5
    first = jnp.arange(nblocks) == 0

    def per_block(items):
        q_blk, k_blk, kp_blk, v_blk, vp_blk, g_blk, leading = items
        usable = jnp.logical_or(column >= BLOCK, jnp.logical_not(leading))

        def per_head(parts):
            q_one, k_one, kp_one, v_one, vp_one, g_one = parts
            return head_pass(q_one, jnp.concatenate([kp_one, k_one], 0), jnp.concatenate([vp_one, v_one], 0), g_one, usable, scale)

        return lax.map(per_head, (q_blk, k_blk, kp_blk, v_blk, vp_blk, g_blk))

    attended_b, query_grad_b, value_terms = lax.map(per_block, (query_b, keys_b, keys_p, values_b, values_p, upstream_b, first))
    prior_part = value_terms[:, :, :BLOCK]
    own_part = value_terms[:, :, BLOCK:]
    incoming = jnp.concatenate([prior_part[1:], jnp.zeros_like(prior_part[:1])], 0)
    value_grad_b = (own_part + incoming).astype(jnp.bfloat16)

    def unblock(array):
        return array.transpose(0, 2, 1, 3).reshape(TOKENS, D)

    attended = unblock(attended_b)
    query_grad = unblock(query_grad_b)
    value_grad = unblock(value_grad_b)
    lowrank = jnp.concatenate([
        jnp.dot(query_grad, up_q.T, preferred_element_type=jnp.float32),
        jnp.dot(value_grad, up_v.T, preferred_element_type=jnp.float32)], 1).astype(jnp.bfloat16)
    down_total = inner(tokens, lowrank)
    grad_down_q = down_total[:, :RANK].astype(jnp.bfloat16)
    grad_down_v = down_total[:, RANK:].astype(jnp.bfloat16)
    grad_up_q = inner(low_q, query_grad).astype(jnp.bfloat16)
    grad_up_v = inner(low_v, value_grad).astype(jnp.bfloat16)
    return attended, grad_down_q, grad_up_q, grad_down_v, grad_up_v
```

```python
import functools

import jax
import jax.numpy as jnp
from jax import lax
from jax.experimental import pallas as pl
from jax.experimental.pallas import tpu as pltpu
from jax.sharding import PartitionSpec as P

HEAD = 128
TILE = 256
LOG2E = 1.4426950408889634
F32 = jnp.float32
BF16 = jnp.bfloat16

Y_CORE = [[half * 16 + z * 2 + core for half in range(2) for core in range(2)] for z in range(8)]
Z_RING = [[half * 16 + z * 2 + core for z in range(8)] for half in range(2) for core in range(2)]


def dot(left, right):
    return jnp.dot(left, right, preferred_element_type=F32)


def dot_t(left, right):
    return lax.dot_general(left, right, (((1,), (1,)), ((), ())), preferred_element_type=F32)


def t_dot(left, right):
    return lax.dot_general(left, right, (((0,), (0,)), ((), ())), preferred_element_type=F32)


def pack_kernel(
    tokens, query_base, key_base, value_base, out_grad, down_q, down_v, up_q, up_v, kvl, qg, low
):
    width = key_base.shape[1]
    rank = down_q.shape[1]

    @pl.when(pl.program_id(0) == 0)
    def _():
        low[:, :rank] = dot(tokens[...], down_q[...]).astype(BF16)
        low[:, rank:] = dot(tokens[...], down_v[...]).astype(BF16)

    kvl[:, :width] = key_base[...]
    kvl[:, width : 2 * width] = (
        value_base[...].astype(F32) + dot(low[:, rank:], up_v[...])
    ).astype(BF16)
    kvl[:, 2 * width :] = low[...]
    qg[:, :width] = (query_base[...].astype(F32) + dot(low[:, :rank], up_q[...])).astype(BF16)
    qg[:, width:] = out_grad[...]


def pack(tokens, query_base, key_base, value_base, out_grad, down_q, up_q, down_v, up_v, parts):
    rows, columns = tokens.shape
    rank = down_q.shape[1]
    width = columns // parts
    whole = lambda j: (0, 0)
    part = lambda j: (0, j)
    once = pl.Buffered(1)
    return pl.pallas_call(
        pack_kernel,
        grid=(parts,),
        in_specs=[pl.BlockSpec((rows, columns), whole, pipeline_mode=once)]
        + [pl.BlockSpec((rows, width), part)] * 4
        + [pl.BlockSpec((columns, rank), whole, pipeline_mode=once)] * 2
        + [pl.BlockSpec((rank, width), part)] * 2,
        out_specs=[
            pl.BlockSpec((rows, 2 * width + 2 * rank), lambda j: (j, 0)),
            pl.BlockSpec((rows, 2 * width), lambda j: (j, 0)),
        ],
        out_shape=[
            jax.ShapeDtypeStruct((parts * rows, 2 * width + 2 * rank), BF16),
            jax.ShapeDtypeStruct((parts * rows, 2 * width), BF16),
        ],
        scratch_shapes=[pltpu.VMEM((rows, 2 * rank), BF16)],
        compiler_params=pltpu.CompilerParams(vmem_limit_bytes=40 << 20),
        name="pack",
    )(tokens, query_base, key_base, value_base, out_grad, down_q, down_v, up_q, up_v)


def attention_kernel(
    place, q, g, k_own, v_own, k_prior, v_prior, low_own, low_prior, up_q, up_v,
    out, ups, lq, lo, lp, dv_own, dv_prior,
):
    head = pl.program_id(0)
    heads = pl.num_programs(0)
    rows = q.shape[0]
    rank = up_q.shape[0]
    scale = HEAD ** (-0.5)
    factor = scale * LOG2E
    has_prior = place[1] > 0

    @pl.when(head == 0)
    def _():
        lq[...] = jnp.zeros_like(lq)
        lo[...] = jnp.zeros_like(lo)
        lp[...] = jnp.zeros_like(lp)

    up_q_grad = jnp.zeros((HEAD, rank), F32)
    for step in range(rows // TILE):
        here = slice(step * TILE, (step + 1) * TILE)
        q_t = q[here, :]
        g_t = g[here, :]
        s_own = dot_t(q_t, k_own[...])
        s_prior = dot_t(q_t, k_prior[...])
        top_own = jnp.max(s_own, axis=1, keepdims=True)
        top_prior = jnp.max(s_prior, axis=1, keepdims=True)
        top = jnp.where(has_prior, jnp.maximum(top_own, top_prior), top_own) * factor
        top_p = jnp.where(has_prior, top, jnp.float32(1e38))
        p_own = jnp.exp2(s_own * factor - top)
        p_prior = jnp.exp2(s_prior * factor - top_p)
        total = jnp.sum(p_own, axis=1, keepdims=True) + jnp.sum(p_prior, axis=1, keepdims=True)
        inverse = 1.0 / total
        p_own = p_own.astype(BF16)
        p_prior = p_prior.astype(BF16)
        attended = ((dot(p_own, v_own[...]) + dot(p_prior, v_prior[...])) * inverse).astype(BF16)
        out[here, pl.ds(pl.multiple_of(head * HEAD, HEAD), HEAD)] = attended
        delta = jnp.sum(g_t.astype(F32) * attended.astype(F32), axis=1, keepdims=True)
        ds_own = (p_own.astype(F32) * (dot_t(g_t, v_own[...]) - delta)).astype(BF16)
        ds_prior = (p_prior.astype(F32) * (dot_t(g_t, v_prior[...]) - delta)).astype(BF16)
        dq = ((dot(ds_own, k_own[...]) + dot(ds_prior, k_prior[...])) * (inverse * scale)).astype(
            BF16
        )
        scaled = (g_t.astype(F32) * inverse).astype(BF16)
        if step == 0:
            dv_own[...] = t_dot(p_own, scaled)
            dv_prior[...] = t_dot(p_prior, scaled)
        else:
            dv_own[...] += t_dot(p_own, scaled)
            dv_prior[...] += t_dot(p_prior, scaled)
        lq[here, :] += dot_t(dq, up_q[...])
        up_q_grad += t_dot(dq, low_own[here, :rank])
    own = dv_own[...].astype(BF16)
    prior = dv_prior[...].astype(BF16)
    lo[...] += dot_t(own, up_v[...])
    lp[...] += dot_t(prior, up_v[...])
    ups[:, :rank] = up_q_grad.astype(BF16)
    ups[:, rank:] = (t_dot(own, low_own[:, rank:]) + t_dot(prior, low_prior[:, rank:])).astype(
        BF16
    )

    @pl.when(head == heads - 1)
    def _():
        width = heads * HEAD
        first = out.shape[1] - 4 * rank
        out[:, first : first + rank] = lq[...].astype(BF16)
        out[:, first + rank : first + 2 * rank] = lo[...].astype(BF16)
        out[:, first + 2 * rank : first + 3 * rank] = lp[...].astype(BF16)
        out[:, first + 3 * rank :] = jnp.zeros((rows, rank), BF16)


def attention(place, qg, kvl, kvl_prior, up_q, up_v):
    rows = qg.shape[0]
    width = qg.shape[1] // 2
    heads = width // HEAD
    rank = up_q.shape[0]
    column = lambda offset: pl.BlockSpec((rows, HEAD), lambda h, place: (0, h + offset))
    fixed = lambda at: pl.BlockSpec((rows, HEAD), lambda h, place: (0, at))
    up = pl.BlockSpec((rank, HEAD), lambda h, place: (0, place[0] * heads + h))
    matmuls = 5 * 2 * heads * rows * 2 * rows * HEAD
    return pl.pallas_call(
        attention_kernel,
        grid_spec=pltpu.PrefetchScalarGridSpec(
            num_scalar_prefetch=1,
            grid=(heads,),
            in_specs=[
                column(0),
                column(heads),
                column(0),
                column(heads),
                column(0),
                column(heads),
                fixed(2 * heads),
                fixed(2 * heads),
                up,
                up,
            ],
            out_specs=[
                pl.BlockSpec((rows, width + 4 * rank), lambda h, place: (0, 0)),
                pl.BlockSpec((HEAD, 2 * rank), lambda h, place: (h, 0)),
            ],
            scratch_shapes=[pltpu.VMEM((rows, rank), F32)] * 3
            + [pltpu.VMEM((rows, HEAD), F32)] * 2,
        ),
        out_shape=[
            jax.ShapeDtypeStruct((rows, width + 4 * rank), BF16),
            jax.ShapeDtypeStruct((width, 2 * rank), BF16),
        ],
        compiler_params=pltpu.CompilerParams(vmem_limit_bytes=56 << 20),
        cost_estimate=pl.CostEstimate(
            flops=matmuls, bytes_accessed=12 << 20, transcendentals=heads * rows * 2 * rows
        ),
        name="attention",
    )(place, qg, qg, kvl, kvl, kvl_prior, kvl_prior, kvl, kvl_prior, up_q, up_v)


def exchange(array, axis, groups=None):
    return lax.all_to_all(
        array, axis, split_axis=0, concat_axis=0, tiled=True, axis_index_groups=groups
    )


def summed(array, axis, size, groups=None):
    got = exchange(array, axis, groups)
    return jnp.sum(got.reshape(size, -1, array.shape[1]).astype(F32), axis=0)


def gathered(array, axis, size, groups=None):
    return exchange(jnp.concatenate([array] * size, 0), axis, groups)


def per_device(tokens, query_base, key_base, value_base, out_grad, down_q, up_q, down_v, up_v):
    blocks = lax.axis_size("blk")
    parts = lax.axis_size("uly")
    rows, columns = tokens.shape
    rank = down_q.shape[1]
    width = columns // parts
    kvl, qg = pack(
        tokens, query_base, key_base, value_base, out_grad, down_q, up_q, down_v, up_v, parts
    )
    kvl = exchange(kvl, "uly")
    kvl_prior = lax.ppermute(kvl, "blk", [(i, i + 1) for i in range(blocks - 1)])
    qg, _ = lax.optimization_barrier((qg, kvl))
    qg = exchange(qg, "uly")
    place = jnp.stack([lax.axis_index("uly"), lax.axis_index("blk")]).astype(jnp.int32)
    out, ups = attention(place, qg, kvl, kvl_prior, up_q, up_v)
    back = exchange(out, "uly").reshape(parts, rows, -1)
    attended = back[:, :, :width].transpose(1, 0, 2).reshape(rows, columns)
    low_terms = jnp.sum(back[:, :, width : width + 3 * rank].astype(F32), axis=0)
    returned = lax.ppermute(
        low_terms[:, 2 * rank :], "blk", [(i, i - 1) for i in range(1, blocks)]
    )
    lowrank = jnp.concatenate(
        [low_terms[:, :rank], low_terms[:, rank : 2 * rank] + returned], 1
    ).astype(BF16)
    down = t_dot(tokens, lowrank).astype(BF16)
    quarter = columns // 4
    both = jnp.concatenate(
        [down.reshape(4, quarter, 2 * rank), ups.reshape(4, width // 4, 2 * rank)], 1
    ).reshape(-1, 2 * rank)
    both = summed(both, "blk", 4, Y_CORE)
    down = summed(both[:quarter].astype(BF16), "uly", parts)
    piece = quarter // parts // 8
    both = jnp.concatenate(
        [down.reshape(8, piece, 2 * rank), both[quarter:].reshape(8, piece, 2 * rank)], 1
    ).reshape(-1, 2 * rank)
    both = summed(both.astype(BF16), "blk", 8, Z_RING).astype(BF16)
    both = gathered(both, "blk", 8, Z_RING).reshape(8, 2 * piece, 2 * rank)
    down = gathered(both[:, :piece].reshape(-1, 2 * rank), "uly", parts)
    ups = both[:, piece:].reshape(-1, 2 * rank)
    both = gathered(jnp.concatenate([down, ups], 0), "blk", 4, Y_CORE).reshape(4, -1, 2 * rank)
    down = both[:, :quarter].reshape(columns, 2 * rank)
    ups = both[:, quarter:].reshape(width, 2 * rank)
    return (
        attended,
        down[:, :rank],
        ups[:, :rank].T,
        down[:, rank:],
        ups[:, rank:].T,
    )


def solution(mesh):
    rows = P(("blk", "uly"), None)
    return jax.shard_map(
        per_device,
        mesh=mesh,
        in_specs=(rows,) * 5 + (P(),) * 4,
        out_specs=(rows, P(), P(None, "uly"), P(), P(None, "uly")),
        check_vma=False,
    )
```

```python
import functools

import jax
import jax.numpy as jnp
from jax import lax
from jax.experimental import pallas as pl
from jax.experimental.pallas import tpu as pltpu
from jax.sharding import PartitionSpec as P

HEAD = 128
TILE = 256
LOG2E = 1.4426950408889634
F32 = jnp.float32
BF16 = jnp.bfloat16
GROUPS = (3, 2)
CALLS = ((2, 1), (2,))

PAIR = [[2 * i, 2 * i + 1] for i in range(16)]
Z_RING = [[half * 16 + z * 2 + core for z in range(8)] for half in range(2) for core in range(2)]
Y_PAIR = [(i, i ^ 16) for i in range(32)]


def dot(left, right):
    return jnp.dot(left, right, preferred_element_type=F32)


def dot_t(left, right):
    return lax.dot_general(left, right, (((1,), (1,)), ((), ())), preferred_element_type=F32)


def t_dot(left, right):
    return lax.dot_general(left, right, (((0,), (0,)), ((), ())), preferred_element_type=F32)


def pack_kernel(
    tokens, query_base, key_base, value_base, out_grad, down_q, down_v, up_q, up_v, *rest
):
    outs, low = rest[:-1], rest[-1]
    rank = down_q.shape[0]

    @pl.when(pl.program_id(0) == 0)
    def _():
        low[:, :rank] = dot_t(tokens[...], down_q[...]).astype(BF16)
        low[:, rank:] = dot_t(tokens[...], down_v[...]).astype(BF16)

    value = (value_base[...].astype(F32) + dot(low[:, rank:], up_v[...])).astype(BF16)
    query = (query_base[...].astype(F32) + dot(low[:, :rank], up_q[...])).astype(BF16)
    first = 0
    for group, heads in enumerate(GROUPS):
        kvl, qg = outs[2 * group], outs[2 * group + 1]
        width = heads * HEAD
        here = slice(first, first + width)
        kvl[:, :width] = key_base[:, here]
        kvl[:, width : 2 * width] = value[:, here]
        if group == 0:
            kvl[:, 2 * width :] = low[...]
        qg[:, :width] = query[:, here]
        qg[:, width:] = out_grad[:, here]
        first += width


def pack(tokens, query_base, key_base, value_base, out_grad, down_q, up_q, down_v, up_v, parts):
    rows, columns = tokens.shape
    rank = down_q.shape[0]
    width = columns // parts
    whole = lambda j: (0, 0)
    part = lambda j: (0, j)
    once = pl.Buffered(1)
    sizes = []
    for group, heads in enumerate(GROUPS):
        sizes += [2 * heads * HEAD + (2 * rank if group == 0 else 0), 2 * heads * HEAD]
    return pl.pallas_call(
        pack_kernel,
        grid=(parts,),
        in_specs=[pl.BlockSpec((rows, columns), whole, pipeline_mode=once)]
        + [pl.BlockSpec((rows, width), part)] * 4
        + [pl.BlockSpec((rank, columns), whole, pipeline_mode=once)] * 2
        + [pl.BlockSpec((rank, width), part)] * 2,
        out_specs=[pl.BlockSpec((rows, size), lambda j: (j, 0)) for size in sizes],
        out_shape=[jax.ShapeDtypeStruct((parts * rows, size), BF16) for size in sizes],
        scratch_shapes=[pltpu.VMEM((rows, 2 * rank), BF16)],
        compiler_params=pltpu.CompilerParams(vmem_limit_bytes=60 << 20),
        cost_estimate=pl.CostEstimate(flops=1 << 29, bytes_accessed=14 << 20, transcendentals=0),
        name="pack",
    )(tokens, query_base, key_base, value_base, out_grad, down_q, down_v, up_q, up_v)


def attention_kernel(
    last, place, q, g, k_own, v_own, k_prior, v_prior, low_own, low_prior, up_q, up_v, low_in,
    buffer, out, ups, *rest,
):
    low_out = None if last else rest[0]
    lq, lo, lp, dv_own, dv_prior = rest[-5:]
    head = pl.program_id(0)
    heads = pl.num_programs(0)
    rows = q.shape[0]
    rank = up_q.shape[0]
    scale = HEAD ** (-0.5)
    factor = scale * LOG2E
    has_prior = place[1] > 0

    @pl.when(head == 0)
    def _():
        lq[...] = low_in[:, :rank]
        lo[...] = low_in[:, rank : 2 * rank]
        lp[...] = low_in[:, 2 * rank : 3 * rank]

    up_q_grad = jnp.zeros((rank, HEAD), F32)
    for step in range(rows // TILE):
        here = slice(step * TILE, (step + 1) * TILE)
        q_t = q[here, :]
        g_t = g[here, :]
        s_own = dot_t(q_t, k_own[...])
        s_prior = dot_t(q_t, k_prior[...])
        top_own = jnp.max(s_own, axis=1, keepdims=True)
        top_prior = jnp.max(s_prior, axis=1, keepdims=True)
        top = jnp.where(has_prior, jnp.maximum(top_own, top_prior), top_own) * factor
        top_p = jnp.where(has_prior, top, jnp.float32(1e38))
        p_own = jnp.exp2(s_own * factor - top)
        p_prior = jnp.exp2(s_prior * factor - top_p)
        total = jnp.sum(p_own, axis=1, keepdims=True) + jnp.sum(p_prior, axis=1, keepdims=True)
        inverse = 1.0 / total
        p_own = p_own.astype(BF16)
        p_prior = p_prior.astype(BF16)
        attended = ((dot(p_own, v_own[...]) + dot(p_prior, v_prior[...])) * inverse).astype(BF16)
        if last:
            out[here, pl.ds(pl.multiple_of(head * HEAD, HEAD), HEAD)] = attended
        else:
            out[here, :] = attended
        delta = jnp.sum(g_t.astype(F32) * attended.astype(F32), axis=1, keepdims=True)
        ds_own = (p_own.astype(F32) * (dot_t(g_t, v_own[...]) - delta)).astype(BF16)
        ds_prior = (p_prior.astype(F32) * (dot_t(g_t, v_prior[...]) - delta)).astype(BF16)
        dq = ((dot(ds_own, k_own[...]) + dot(ds_prior, k_prior[...])) * (inverse * scale)).astype(
            BF16
        )
        scaled = (g_t.astype(F32) * inverse).astype(BF16)
        if step == 0:
            dv_own[...] = t_dot(p_own, scaled)
            dv_prior[...] = t_dot(p_prior, scaled)
        else:
            dv_own[...] += t_dot(p_own, scaled)
            dv_prior[...] += t_dot(p_prior, scaled)
        lq[here, :] += dot_t(dq, up_q[...])
        up_q_grad += t_dot(low_own[here, :rank], dq)
    own = dv_own[...].astype(BF16)
    prior = dv_prior[...].astype(BF16)
    lo[...] += dot_t(own, up_v[...])
    lp[...] += dot_t(prior, up_v[...])
    ups[0] = up_q_grad.astype(BF16)
    ups[1] = (t_dot(low_own[:, rank:], own) + t_dot(low_prior[:, rank:], prior)).astype(BF16)

    @pl.when(head == heads - 1)
    def _():
        to = out if last else low_out
        first = to.shape[1] - 4 * rank
        to[:, first : first + rank] = lq[...].astype(to.dtype)
        to[:, first + rank : first + 2 * rank] = lo[...].astype(to.dtype)
        to[:, first + 2 * rank : first + 3 * rank] = lp[...].astype(to.dtype)
        to[:, first + 3 * rank :] = jnp.zeros((rows, rank), to.dtype)


def attention(place, qg, kvl, kvl_prior, low, low_prior, up_q, up_v, low_in, buffer, at, heads, last):
    rows = qg.shape[0]
    width = qg.shape[1] // 2
    held = width // HEAD
    rank = up_q.shape[0]
    total = sum(GROUPS)
    group_first, first = at
    column = lambda offset: pl.BlockSpec((rows, HEAD), lambda h, place: (0, h + offset))
    fixed = pl.BlockSpec((rows, HEAD), lambda h, place: (0, 2 * GROUPS[0]))
    up = pl.BlockSpec(
        (rank, HEAD), lambda h, place: (0, place[0] * total + group_first + first + h)
    )
    lows = pl.BlockSpec((rows, 4 * rank), lambda h, place: (0, 0))
    out_width = width + 4 * rank if last else width
    out_specs = [
        pl.BlockSpec((rows, out_width), lambda h, place: (0, 0)) if last else column(first),
        pl.BlockSpec((2, rank, HEAD), lambda h, place: (0, h, 0)),
    ]
    out_shape = [
        jax.ShapeDtypeStruct((rows, out_width), BF16),
        jax.ShapeDtypeStruct((2, heads * rank, HEAD), BF16),
    ]
    if not last:
        out_specs.append(lows)
        out_shape.append(jax.ShapeDtypeStruct((rows, 4 * rank), F32))
    aliases = {12: 0}
    if buffer is None:
        buffer = place
        aliases = {}
    return pl.pallas_call(
        functools.partial(attention_kernel, last),
        grid_spec=pltpu.PrefetchScalarGridSpec(
            num_scalar_prefetch=1,
            grid=(heads,),
            in_specs=[
                column(first),
                column(held + first),
                column(first),
                column(held + first),
                column(first),
                column(held + first),
                fixed,
                fixed,
                up,
                up,
                lows,
                pl.BlockSpec(memory_space=pl.ANY),
            ],
            out_specs=out_specs,
            scratch_shapes=[pltpu.VMEM((rows, rank), F32)] * 3
            + [pltpu.VMEM((rows, HEAD), F32)] * 2,
        ),
        out_shape=out_shape,
        input_output_aliases=aliases,
        compiler_params=pltpu.CompilerParams(vmem_limit_bytes=60 << 20),
        cost_estimate=pl.CostEstimate(
            flops=5 * 2 * heads * rows * 2 * rows * HEAD * 4,
            bytes_accessed=heads << 21,
            transcendentals=heads * rows * 2 * rows,
        ),
        name="attention",
    )(place, qg, qg, kvl, kvl, kvl_prior, kvl_prior, low, low_prior, up_q, up_v, low_in, buffer)


def outer_kernel(lows, tokens, earlier, *rest):
    ups, out = rest[:-2], rest[-1]
    rows, columns = tokens.shape
    rank = lows.shape[1] // 4
    low = jnp.sum(lows[...].reshape(-1, rows, 4 * rank).astype(F32), axis=0).astype(BF16)
    grad_q = t_dot(low[:, :rank], tokens[...])
    grad_v = t_dot(low[:, rank : 2 * rank], tokens[...]) + t_dot(
        low[:, 2 * rank : 3 * rank], earlier[...]
    )
    for block in range(columns // HEAD):
        to = slice(block * rank, (block + 1) * rank)
        out[0, to, :] = grad_q[:, block * HEAD : (block + 1) * HEAD].astype(BF16)
        out[1, to, :] = grad_v[:, block * HEAD : (block + 1) * HEAD].astype(BF16)
    first = columns // HEAD * rank
    for up in ups:
        size = up.shape[1]
        out[:, first : first + size, :] = up[...]
        first += size


def outer(lows, tokens, earlier, ups, rank, settled):
    length = tokens.shape[1] // HEAD * rank + sum(up.shape[1] for up in ups)
    whole = lambda array: pl.BlockSpec(array.shape, lambda i: (0,) * array.ndim)
    at = lows.shape[1] // (4 * rank) - 1
    return pl.pallas_call(
        outer_kernel,
        grid=(1,),
        in_specs=[pl.BlockSpec((lows.shape[0], 4 * rank), lambda i: (0, at))]
        + [whole(array) for array in (tokens, earlier, *ups)]
        + [pl.BlockSpec(memory_space=pl.ANY)],
        out_specs=pl.BlockSpec((2, length, HEAD), lambda i: (0, 0, 0)),
        out_shape=jax.ShapeDtypeStruct((2, length, HEAD), BF16),
        compiler_params=pltpu.CompilerParams(vmem_limit_bytes=60 << 20),
        cost_estimate=pl.CostEstimate(flops=1 << 29, bytes_accessed=8 << 20, transcendentals=0),
        name="outer",
    )(lows, tokens, earlier, *ups, settled)


def unpack_kernel(both, down_q, down_v, up_q, up_v):
    rank, columns = down_q.shape
    first = columns // HEAD * rank
    for part, (down, up) in enumerate(((down_q, up_q), (down_v, up_v))):
        for block in range(columns // HEAD):
            down[:, block * HEAD : (block + 1) * HEAD] = both[
                part, block * rank : (block + 1) * rank, :
            ]
        for block in range(up.shape[1] // HEAD):
            up[:, block * HEAD : (block + 1) * HEAD] = both[
                part, first + block * rank : first + (block + 1) * rank, :
            ]


def unpack(both, rank, columns, width):
    return pl.pallas_call(
        unpack_kernel,
        out_shape=[jax.ShapeDtypeStruct((rank, columns), BF16)] * 2
        + [jax.ShapeDtypeStruct((rank, width), BF16)] * 2,
        compiler_params=pltpu.CompilerParams(vmem_limit_bytes=60 << 20),
        name="unpack",
    )(both)


def exchange(array, axis, groups=None):
    return lax.all_to_all(
        array, axis, split_axis=0, concat_axis=0, tiled=True, axis_index_groups=groups
    )


def summed(array, axis, size, groups=None):
    got = exchange(array, axis, groups)
    return jnp.sum(got.reshape(size, -1, array.shape[1]).astype(F32), axis=0).astype(BF16)


def gathered(array, axis, size, groups=None):
    copies = jnp.broadcast_to(array[None], (size,) + array.shape)
    return exchange(copies.reshape(-1, array.shape[1]), axis, groups)


def after(array, *others):
    return pl.pallas_call(
        lambda *refs: None,
        in_specs=[pl.BlockSpec(memory_space=pl.ANY)] * (1 + len(others)),
        out_specs=pl.BlockSpec(memory_space=pl.ANY),
        out_shape=jax.ShapeDtypeStruct(array.shape, array.dtype),
        input_output_aliases={0: 0},
        name="after",
    )(array, *others)


def per_device(tokens, query_base, key_base, value_base, out_grad, down_q, up_q, down_v, up_v):
    blocks = lax.axis_size("blk")
    parts = lax.axis_size("uly")
    rows, columns = tokens.shape
    rank = down_q.shape[1]
    width = columns // parts
    forward = [(i, i + 1) for i in range(blocks - 1)]
    packed = pack(
        tokens, query_base, key_base, value_base, out_grad, down_q.T, up_q, down_v.T, up_v, parts
    )
    place = jnp.stack([lax.axis_index("uly"), lax.axis_index("blk")]).astype(jnp.int32)
    lows = jnp.zeros((parts * rows, 4 * rank), F32)

    def calls(group, received, low, lows):
        kvl, prior, qg = received
        out, ups, first = None, [], 0
        for heads in CALLS[group]:
            last = group == len(GROUPS) - 1
            result = attention(
                place, qg, kvl, prior, *low, up_q, up_v, lows, out,
                (sum(GROUPS[:group]), first), heads, last,
            )
            out = result[0]
            ups.append(result[1])
            lows = None if last else result[2]
            first += heads
            yield out, ups, lows

    kvl_a = exchange(packed[0], "uly")
    prior_a = lax.ppermute(kvl_a, "blk", forward)
    qg_a = exchange(after(packed[1], kvl_a), "uly")
    low = (kvl_a, prior_a)
    kvl_b = exchange(after(packed[2], prior_a, qg_a), "uly")
    run = calls(0, (kvl_a, prior_a, qg_a), low, lows)
    out, ups, lows = next(run)
    kvl_b = after(kvl_b, out)
    prior_b = lax.ppermute(kvl_b, "blk", forward)
    qg_b = exchange(after(packed[3], kvl_b), "uly")
    earlier = lax.ppermute(tokens, "blk", forward)
    out_a, ups, lows = next(run)
    piece_a = exchange(out_a, "uly")
    out_b, ups_b, _ = next(calls(1, (kvl_b, prior_b, qg_b), low, lows))
    back = exchange(out_b, "uly")
    pieces = [piece_a, back]
    both = outer(back, tokens, earlier, ups + ups_b, rank, piece_a)
    both = summed(both.reshape(-1, HEAD), "blk", 2, PAIR)
    length = columns // HEAD * rank
    down = summed(both[:length], "uly", parts)
    piece = length // parts // 8
    both = jnp.concatenate(
        [down.reshape(8, piece, HEAD), both[length:].reshape(8, -1, HEAD)], 1
    ).reshape(-1, HEAD)
    both = summed(both, "blk", 8, Z_RING)
    both = (both.astype(F32) + lax.ppermute(both, "blk", Y_PAIR).astype(F32)).astype(BF16)
    both = gathered(both, "blk", 8, Z_RING).reshape(8, -1, HEAD)
    down = gathered(both[:, :piece].reshape(-1, HEAD), "uly", parts)
    both = jnp.concatenate([down, both[:, piece:].reshape(-1, HEAD)], 0)
    both = gathered(both, "blk", 2, PAIR).reshape(2, -1, HEAD)
    down_q, down_v, up_q, up_v = unpack(both, rank, columns, width)
    attended = jnp.concatenate(
        [
            p.reshape(parts, rows, -1)[:, :, : heads * HEAD]
            for p, heads in zip(pieces, GROUPS)
        ],
        2,
    )
    attended = attended.transpose(1, 0, 2).reshape(rows, columns)
    return (attended, down_q.T, up_q, down_v.T, up_v)


def solution(mesh):
    rows = P(("blk", "uly"), None)
    return jax.shard_map(
        per_device,
        mesh=mesh,
        in_specs=(rows,) * 5 + (P(),) * 4,
        out_specs=(rows, P(), P(None, "uly"), P(), P(None, "uly")),
        check_vma=False,
    )
```

```python
import functools

import jax
import jax.numpy as jnp
from jax import lax
from jax.experimental import pallas as pl
from jax.experimental.pallas import tpu as pltpu
from jax.sharding import PartitionSpec as P

HEAD = 128
TILE = 256
LOG2E = 1.4426950408889634
F32 = jnp.float32
BF16 = jnp.bfloat16
CALLS = (3, 2)

PAIR = [[2 * i, 2 * i + 1] for i in range(16)]
Z_RING = [[half * 16 + z * 2 + core for z in range(8)] for half in range(2) for core in range(2)]
Y_PAIR = [(i, i ^ 16) for i in range(32)]


def dot(left, right):
    return jnp.dot(left, right, preferred_element_type=F32)


def dot_t(left, right):
    return lax.dot_general(left, right, (((1,), (1,)), ((), ())), preferred_element_type=F32)


def t_dot(left, right):
    return lax.dot_general(left, right, (((0,), (0,)), ((), ())), preferred_element_type=F32)


def spread_kernel(array, out):
    out[...] = array[...]


def spread(array, parts):
    rows, columns = array.shape
    width = columns // parts
    return pl.pallas_call(
        spread_kernel,
        grid=(parts,),
        in_specs=[pl.BlockSpec((rows, width), lambda j: (0, j))],
        out_specs=pl.BlockSpec((rows, width), lambda j: (j, 0)),
        out_shape=jax.ShapeDtypeStruct((parts * rows, width), BF16),
        compiler_params=pltpu.CompilerParams(vmem_limit_bytes=60 << 20),
        name="spread",
    )(array)


def pack_kernel(
    tokens, query_base, value_base, out_grad, down_q, down_v, up_q, up_v, vl, qg, copy, low
):
    rank = down_q.shape[0]
    width = value_base.shape[1]

    @pl.when(pl.program_id(0) == 0)
    def _():
        low[:, :rank] = dot_t(tokens[...], down_q[...]).astype(BF16)
        low[:, rank:] = dot_t(tokens[...], down_v[...]).astype(BF16)
        copy[...] = tokens[...]

    vl[:, :width] = (value_base[...].astype(F32) + dot(low[:, rank:], up_v[...])).astype(BF16)
    vl[:, width:] = low[...]
    qg[:, :width] = (query_base[...].astype(F32) + dot(low[:, :rank], up_q[...])).astype(BF16)
    qg[:, width:] = out_grad[...]


def pack(tokens, query_base, value_base, out_grad, down_q, up_q, down_v, up_v, parts):
    rows, columns = tokens.shape
    rank = down_q.shape[0]
    width = columns // parts
    whole = lambda j: (0, 0)
    part = lambda j: (0, j)
    once = pl.Buffered(1)
    sizes = (width + 2 * rank, 2 * width)
    return pl.pallas_call(
        pack_kernel,
        grid=(parts,),
        in_specs=[pl.BlockSpec((rows, columns), whole, pipeline_mode=once)]
        + [pl.BlockSpec((rows, width), part)] * 3
        + [pl.BlockSpec((rank, columns), whole, pipeline_mode=once)] * 2
        + [pl.BlockSpec((rank, width), part)] * 2,
        out_specs=[pl.BlockSpec((rows, size), lambda j: (j, 0)) for size in sizes]
        + [pl.BlockSpec((rows, columns), whole)],
        out_shape=[jax.ShapeDtypeStruct((parts * rows, size), BF16) for size in sizes]
        + [jax.ShapeDtypeStruct((rows, columns), BF16)],
        scratch_shapes=[pltpu.VMEM((rows, 2 * rank), BF16)],
        compiler_params=pltpu.CompilerParams(vmem_limit_bytes=60 << 20),
        cost_estimate=pl.CostEstimate(flops=1 << 29, bytes_accessed=14 << 20, transcendentals=0),
        name="pack",
    )(tokens, query_base, value_base, out_grad, down_q, down_v, up_q, up_v)


def attention_kernel(
    begins, ends, place, q, g, k_own, v_own, k_prior, v_prior, low_own, low_prior, up_q, up_v, *rest
):
    rest = list(rest)
    low_in = None if begins else [rest.pop(0) for _ in range(3)]
    out, ups = rest.pop(0), rest.pop(0)
    low_out = None if ends else [rest.pop(0) for _ in range(3)]
    lq, lo, lp, dv_own, dv_prior = rest
    head = pl.program_id(0)
    heads = pl.num_programs(0)
    rows = q.shape[0]
    rank = up_q.shape[0]
    scale = HEAD ** (-0.5)
    factor = scale * LOG2E
    has_prior = place[1] > 0

    @pl.when(head == 0)
    def _():
        if begins:
            lq[...] = jnp.zeros_like(lq)
            lo[...] = jnp.zeros_like(lo)
            lp[...] = jnp.zeros_like(lp)
        else:
            lq[...] = low_in[0][...]
            lo[...] = low_in[1][...]
            lp[...] = low_in[2][...]

    def softmax(step):
        here = slice(step * TILE, (step + 1) * TILE)
        q_t = q[here, :]
        s_own = dot_t(q_t, k_own[...])
        s_prior = dot_t(q_t, k_prior[...])
        top_own = jnp.max(s_own, axis=1, keepdims=True)
        top_prior = jnp.max(s_prior, axis=1, keepdims=True)
        top = jnp.where(has_prior, jnp.maximum(top_own, top_prior), top_own) * factor
        top_p = jnp.where(has_prior, top, jnp.float32(1e38))
        p_own = jnp.exp2(s_own * factor - top)
        p_prior = jnp.exp2(s_prior * factor - top_p)
        total = jnp.sum(p_own, axis=1, keepdims=True) + jnp.sum(p_prior, axis=1, keepdims=True)
        return here, p_own.astype(BF16), p_prior.astype(BF16), 1.0 / total

    up_q_grad = jnp.zeros((rank, HEAD), F32)
    steps = rows // TILE
    following = softmax(0)
    for step in range(steps):
        here, p_own, p_prior, inverse = following
        if step + 1 < steps:
            following = softmax(step + 1)
        g_t = g[here, :]
        attended = ((dot(p_own, v_own[...]) + dot(p_prior, v_prior[...])) * inverse).astype(BF16)
        if ends:
            out[here, pl.ds(pl.multiple_of(head * HEAD, HEAD), HEAD)] = attended
        else:
            out[here, :] = attended
        delta = jnp.sum(g_t.astype(F32) * attended.astype(F32), axis=1, keepdims=True)
        ds_own = (p_own.astype(F32) * (dot_t(g_t, v_own[...]) - delta)).astype(BF16)
        ds_prior = (p_prior.astype(F32) * (dot_t(g_t, v_prior[...]) - delta)).astype(BF16)
        dq = ((dot(ds_own, k_own[...]) + dot(ds_prior, k_prior[...])) * (inverse * scale)).astype(
            BF16
        )
        scaled = (g_t.astype(F32) * inverse).astype(BF16)
        if step == 0:
            dv_own[...] = t_dot(scaled, p_own)
            dv_prior[...] = t_dot(scaled, p_prior)
        else:
            dv_own[...] += t_dot(scaled, p_own)
            dv_prior[...] += t_dot(scaled, p_prior)
        lq[here, :] += dot_t(dq, up_q[...])
        up_q_grad += t_dot(low_own[here, :rank], dq)
    own = dv_own[...].astype(BF16)
    prior = dv_prior[...].astype(BF16)
    lo[...] += dot(up_v[...], own)
    lp[...] += dot(up_v[...], prior)
    ups[0] = up_q_grad.astype(BF16)
    ups[1] = (dot(own, low_own[:, rank:]) + dot(prior, low_prior[:, rank:])).T.astype(BF16)

    @pl.when(head == heads - 1)
    def _():
        if ends:
            first = out.shape[1] - 4 * rank
            out[:, first : first + rank] = lq[...].astype(BF16)
            out[:, first + rank : first + 2 * rank] = lo[...].T.astype(BF16)
            out[:, first + 2 * rank : first + 3 * rank] = lp[...].T.astype(BF16)
            out[:, first + 3 * rank :] = jnp.zeros((rows, rank), BF16)
        else:
            low_out[0][...] = lq[...]
            low_out[1][...] = lo[...]
            low_out[2][...] = lp[...]


def attention(place, qg, k, k_prior, vl, vl_prior, up_q, up_v, lows, first, heads, ends):
    rows = qg.shape[0]
    total = k.shape[1] // HEAD
    rank = up_q.shape[0]
    begins = lows is None
    column = lambda offset: pl.BlockSpec((rows, HEAD), lambda h, place: (0, first + h + offset))
    fixed = pl.BlockSpec((rows, HEAD), lambda h, place: (0, total))
    up = pl.BlockSpec((rank, HEAD), lambda h, place: (0, place[0] * total + first + h))
    shapes = ((rows, rank), (rank, rows), (rank, rows))
    whole = lambda shape: pl.BlockSpec(shape, lambda h, place: (0, 0))
    width = heads * HEAD
    out_width = width + 4 * rank if ends else width
    out_specs = [
        whole((rows, out_width)) if ends else pl.BlockSpec((rows, HEAD), lambda h, place: (0, h)),
        pl.BlockSpec((2, rank, HEAD), lambda h, place: (0, h, 0)),
    ]
    out_shape = [
        jax.ShapeDtypeStruct((rows, out_width), BF16),
        jax.ShapeDtypeStruct((2, heads * rank, HEAD), BF16),
    ]
    if not ends:
        out_specs += [whole(shape) for shape in shapes]
        out_shape += [jax.ShapeDtypeStruct(shape, F32) for shape in shapes]
    return pl.pallas_call(
        functools.partial(attention_kernel, begins, ends),
        grid_spec=pltpu.PrefetchScalarGridSpec(
            num_scalar_prefetch=1,
            grid=(heads,),
            in_specs=[
                column(0),
                column(total),
                column(0),
                column(0),
                column(0),
                column(0),
                fixed,
                fixed,
                up,
                up,
            ]
            + ([] if begins else [whole(shape) for shape in shapes]),
            out_specs=out_specs,
            scratch_shapes=[pltpu.VMEM(shape, F32) for shape in shapes]
            + [pltpu.VMEM((HEAD, rows), F32)] * 2,
        ),
        out_shape=out_shape,
        compiler_params=pltpu.CompilerParams(vmem_limit_bytes=60 << 20),
        cost_estimate=pl.CostEstimate(
            flops=5 * 2 * heads * rows * 2 * rows * HEAD * 4,
            bytes_accessed=heads << 21,
            transcendentals=heads * rows * 2 * rows,
        ),
        name="attention",
    )(
        place, qg, qg, k, vl, k_prior, vl_prior, vl, vl_prior, up_q, up_v,
        *(() if begins else lows),
    )


def outer_kernel(lows, tokens, earlier, *rest):
    ups, out = rest[:-2], rest[-1]
    rows, columns = tokens.shape
    rank = lows.shape[1] // 4
    low = jnp.sum(lows[...].reshape(-1, rows, 4 * rank).astype(F32), axis=0).astype(BF16)
    grad_q = t_dot(low[:, :rank], tokens[...])
    grad_v = t_dot(low[:, rank : 2 * rank], tokens[...]) + t_dot(
        low[:, 2 * rank : 3 * rank], earlier[...]
    )
    for block in range(columns // HEAD):
        to = slice(block * rank, (block + 1) * rank)
        out[0, to, :] = grad_q[:, block * HEAD : (block + 1) * HEAD].astype(BF16)
        out[1, to, :] = grad_v[:, block * HEAD : (block + 1) * HEAD].astype(BF16)
    first = columns // HEAD * rank
    for up in ups:
        size = up.shape[1]
        out[:, first : first + size, :] = up[...]
        first += size


def outer(lows, tokens, earlier, ups, rank, settled):
    length = tokens.shape[1] // HEAD * rank + sum(up.shape[1] for up in ups)
    whole = lambda array: pl.BlockSpec(array.shape, lambda i: (0,) * array.ndim)
    at = lows.shape[1] // (4 * rank) - 1
    return pl.pallas_call(
        outer_kernel,
        grid=(1,),
        in_specs=[pl.BlockSpec((lows.shape[0], 4 * rank), lambda i: (0, at))]
        + [whole(array) for array in (tokens, earlier, *ups)]
        + [pl.BlockSpec(memory_space=pl.ANY)],
        out_specs=pl.BlockSpec((2, length, HEAD), lambda i: (0, 0, 0)),
        out_shape=jax.ShapeDtypeStruct((2, length, HEAD), BF16),
        compiler_params=pltpu.CompilerParams(vmem_limit_bytes=60 << 20),
        cost_estimate=pl.CostEstimate(flops=1 << 29, bytes_accessed=8 << 20, transcendentals=0),
        name="outer",
    )(lows, tokens, earlier, *ups, settled)


def unpack_kernel(both, down_q, down_v, up_q, up_v):
    rank, columns = down_q.shape
    first = columns // HEAD * rank
    for part, (down, up) in enumerate(((down_q, up_q), (down_v, up_v))):
        for block in range(columns // HEAD):
            down[:, block * HEAD : (block + 1) * HEAD] = both[
                part, block * rank : (block + 1) * rank, :
            ]
        for block in range(up.shape[1] // HEAD):
            up[:, block * HEAD : (block + 1) * HEAD] = both[
                part, first + block * rank : first + (block + 1) * rank, :
            ]


def unpack(both, rank, columns, width):
    return pl.pallas_call(
        unpack_kernel,
        out_shape=[jax.ShapeDtypeStruct((rank, columns), BF16)] * 2
        + [jax.ShapeDtypeStruct((rank, width), BF16)] * 2,
        compiler_params=pltpu.CompilerParams(vmem_limit_bytes=60 << 20),
        name="unpack",
    )(both)


def exchange(array, axis, groups=None):
    return lax.all_to_all(
        array, axis, split_axis=0, concat_axis=0, tiled=True, axis_index_groups=groups
    )


def summed(array, axis, size, groups=None):
    got = exchange(array, axis, groups)
    return jnp.sum(got.reshape(size, -1, array.shape[1]).astype(F32), axis=0).astype(BF16)


def gathered(array, axis, size, groups=None):
    copies = jnp.broadcast_to(array[None], (size,) + array.shape)
    return exchange(copies.reshape(-1, array.shape[1]), axis, groups)


def after(array, *others):
    return pl.pallas_call(
        lambda *refs: None,
        in_specs=[pl.BlockSpec(memory_space=pl.ANY)] * (1 + len(others)),
        out_specs=pl.BlockSpec(memory_space=pl.ANY),
        out_shape=jax.ShapeDtypeStruct(array.shape, array.dtype),
        input_output_aliases={0: 0},
        name="after",
    )(array, *others)


def shifted(array, blocks):
    wrap = blocks // 2 - 1
    half = array.shape[0] // 2
    direct = lax.ppermute(
        array, "blk", [(i, i + 1) for i in range(blocks - 1) if i != wrap]
    )
    upper = lax.ppermute(array[:half], "blk", [(wrap, wrap + 1)])
    lower = lax.ppermute(array[half:], "blk", [(wrap, blocks - 1)])
    lower = lax.ppermute(lower, "blk", [(blocks - 1, wrap + 1)])
    return direct + jnp.concatenate([upper, lower], 0)


def per_device(tokens, query_base, key_base, value_base, out_grad, down_q, up_q, down_v, up_v):
    blocks = lax.axis_size("blk")
    parts = lax.axis_size("uly")
    rows, columns = tokens.shape
    rank = down_q.shape[1]
    width = columns // parts
    vl, qg, copy = pack(
        tokens, query_base, value_base, out_grad, down_q.T, up_q, down_v.T, up_v, parts
    )
    k = exchange(spread(key_base, parts), "uly")
    k_prior = shifted(k, blocks)
    vl = exchange(vl, "uly")
    vl_prior = shifted(vl, blocks)
    qg = exchange(after(qg, vl), "uly")
    earlier = lax.ppermute(
        after(copy, vl_prior), "blk", [(i, i + 1) for i in range(blocks - 1)]
    )
    place = jnp.stack([lax.axis_index("uly"), lax.axis_index("blk")]).astype(jnp.int32)
    ready = (place, qg, k, k_prior, vl, vl_prior, up_q, up_v)
    out, ups_a, *lows = attention(*ready, None, 0, CALLS[0], False)
    piece = exchange(out, "uly")
    out, ups_b = attention(*ready, lows, CALLS[0], CALLS[1], True)
    back = exchange(out, "uly")
    pieces = (piece, back)
    both = outer(back, tokens, earlier, (ups_a, ups_b), rank, piece)
    both = summed(both.reshape(-1, HEAD), "blk", 2, PAIR)
    length = columns // HEAD * rank
    down = summed(both[:length], "uly", parts)
    piece = length // parts // 8
    both = jnp.concatenate(
        [down.reshape(8, piece, HEAD), both[length:].reshape(8, -1, HEAD)], 1
    ).reshape(-1, HEAD)
    both = summed(both, "blk", 8, Z_RING)
    both = (both.astype(F32) + lax.ppermute(both, "blk", Y_PAIR).astype(F32)).astype(BF16)
    both = gathered(both, "blk", 8, Z_RING).reshape(8, -1, HEAD)
    down = gathered(both[:, :piece].reshape(-1, HEAD), "uly", parts)
    both = jnp.concatenate([down, both[:, piece:].reshape(-1, HEAD)], 0)
    both = gathered(both, "blk", 2, PAIR).reshape(2, -1, HEAD)
    down_q, down_v, up_q, up_v = unpack(both, rank, columns, width)
    attended = jnp.concatenate(
        [
            p.reshape(parts, rows, -1)[:, :, : heads * HEAD]
            for p, heads in zip(pieces, CALLS)
        ],
        2,
    )
    attended = attended.transpose(1, 0, 2).reshape(rows, columns)
    return (attended, down_q.T, up_q, down_v.T, up_v)


def solution(mesh):
    rows = P(("blk", "uly"), None)
    return jax.shard_map(
        per_device,
        mesh=mesh,
        in_specs=(rows,) * 5 + (P(),) * 4,
        out_specs=(rows, P(), P(None, "uly"), P(), P(None, "uly")),
        check_vma=False,
    )
```

```python
import functools

import jax
import jax.numpy as jnp
from jax import lax
from jax.experimental import pallas as pl
from jax.experimental.pallas import tpu as pltpu
from jax.sharding import PartitionSpec as P

HEAD = 128
TILE = 256
LOG2E = 1.4426950408889634
F32 = jnp.float32
BF16 = jnp.bfloat16
CALLS = (3, 2)

PAIR = [[2 * i, 2 * i + 1] for i in range(16)]
Z_RING = [[half * 16 + z * 2 + core for z in range(8)] for half in range(2) for core in range(2)]
Y_PAIR = [(i, i ^ 16) for i in range(32)]


def dot(left, right):
    return jnp.dot(left, right, preferred_element_type=F32)


def dot_t(left, right):
    return lax.dot_general(left, right, (((1,), (1,)), ((), ())), preferred_element_type=F32)


def t_dot(left, right):
    return lax.dot_general(left, right, (((0,), (0,)), ((), ())), preferred_element_type=F32)


def pack_kernel(
    tokens, query_base, value_base, out_grad, down_q, down_v, up_q, up_v, vl, *rest
):
    qgs, copy, low = rest[:-2], rest[-2], rest[-1]
    rank = down_q.shape[0]
    width = value_base.shape[1]

    @pl.when(pl.program_id(0) == 0)
    def _():
        low[:, :rank] = dot_t(tokens[...], down_q[...]).astype(BF16)
        low[:, rank:] = dot_t(tokens[...], down_v[...]).astype(BF16)
        copy[...] = tokens[...]

    vl[:, :width] = (value_base[...].astype(F32) + dot(low[:, rank:], up_v[...])).astype(BF16)
    vl[:, width:] = low[...]
    query = (query_base[...].astype(F32) + dot(low[:, :rank], up_q[...])).astype(BF16)
    first = 0
    for qg, heads in zip(qgs, CALLS):
        part = heads * HEAD
        qg[:, :part] = query[:, first : first + part]
        qg[:, part:] = out_grad[:, first : first + part]
        first += part


def pack(tokens, query_base, value_base, out_grad, down_q, up_q, down_v, up_v, parts):
    rows, columns = tokens.shape
    rank = down_q.shape[0]
    width = columns // parts
    whole = lambda j: (0, 0)
    part = lambda j: (0, j)
    once = pl.Buffered(1)
    sizes = [width + 2 * rank] + [2 * heads * HEAD for heads in CALLS]
    return pl.pallas_call(
        pack_kernel,
        grid=(parts,),
        in_specs=[pl.BlockSpec((rows, columns), whole, pipeline_mode=once)]
        + [pl.BlockSpec((rows, width), part)] * 3
        + [pl.BlockSpec((rank, columns), whole, pipeline_mode=once)] * 2
        + [pl.BlockSpec((rank, width), part)] * 2,
        out_specs=[pl.BlockSpec((rows, size), lambda j: (j, 0)) for size in sizes]
        + [pl.BlockSpec((rows, columns), whole)],
        out_shape=[jax.ShapeDtypeStruct((parts * rows, size), BF16) for size in sizes]
        + [jax.ShapeDtypeStruct((rows, columns), BF16)],
        scratch_shapes=[pltpu.VMEM((rows, 2 * rank), BF16)],
        compiler_params=pltpu.CompilerParams(vmem_limit_bytes=60 << 20),
        cost_estimate=pl.CostEstimate(flops=1 << 29, bytes_accessed=14 << 20, transcendentals=0),
        name="pack",
    )(tokens, query_base, value_base, out_grad, down_q, down_v, up_q, up_v)


def attention_kernel(
    begins, ends, place, q, g, k_own, v_own, k_prior, v_prior, low_own, low_prior, up_q, up_v, *rest
):
    rest = list(rest)
    low_in = None if begins else [rest.pop(0) for _ in range(3)]
    out, ups = rest.pop(0), rest.pop(0)
    low_out = None if ends else [rest.pop(0) for _ in range(3)]
    lq, lo, lp, dv_own, dv_prior = rest
    head = pl.program_id(0)
    heads = pl.num_programs(0)
    rows = q.shape[0]
    rank = up_q.shape[0]
    scale = HEAD ** (-0.5)
    factor = scale * LOG2E
    has_prior = place[1] > 0

    @pl.when(head == 0)
    def _():
        if begins:
            lq[...] = jnp.zeros_like(lq)
            lo[...] = jnp.zeros_like(lo)
            lp[...] = jnp.zeros_like(lp)
        else:
            lq[...] = low_in[0][...]
            lo[...] = low_in[1][...]
            lp[...] = low_in[2][...]

    def softmax(step):
        here = slice(step * TILE, (step + 1) * TILE)
        q_t = q[here, :]
        s_own = dot_t(q_t, k_own[...])
        s_prior = dot_t(q_t, k_prior[...])
        top_own = jnp.max(s_own, axis=1, keepdims=True)
        top_prior = jnp.max(s_prior, axis=1, keepdims=True)
        top = jnp.where(has_prior, jnp.maximum(top_own, top_prior), top_own) * factor
        top_p = jnp.where(has_prior, top, jnp.float32(1e38))
        p_own = jnp.exp2(s_own * factor - top)
        p_prior = jnp.exp2(s_prior * factor - top_p)
        total = jnp.sum(p_own, axis=1, keepdims=True) + jnp.sum(p_prior, axis=1, keepdims=True)
        return here, p_own.astype(BF16), p_prior.astype(BF16), 1.0 / total

    up_q_grad = jnp.zeros((rank, HEAD), F32)
    steps = rows // TILE
    following = softmax(0)
    for step in range(steps):
        here, p_own, p_prior, inverse = following
        if step + 1 < steps:
            following = softmax(step + 1)
        g_t = g[here, :]
        attended = ((dot(p_own, v_own[...]) + dot(p_prior, v_prior[...])) * inverse).astype(BF16)
        if ends:
            out[here, pl.ds(pl.multiple_of(head * HEAD, HEAD), HEAD)] = attended
        else:
            out[here, :] = attended
        delta = jnp.sum(g_t.astype(F32) * attended.astype(F32), axis=1, keepdims=True)
        ds_own = (p_own.astype(F32) * (dot_t(g_t, v_own[...]) - delta)).astype(BF16)
        ds_prior = (p_prior.astype(F32) * (dot_t(g_t, v_prior[...]) - delta)).astype(BF16)
        dq = ((dot(ds_own, k_own[...]) + dot(ds_prior, k_prior[...])) * (inverse * scale)).astype(
            BF16
        )
        scaled = (g_t.astype(F32) * inverse).astype(BF16)
        if step == 0:
            dv_own[...] = t_dot(scaled, p_own)
            dv_prior[...] = t_dot(scaled, p_prior)
        else:
            dv_own[...] += t_dot(scaled, p_own)
            dv_prior[...] += t_dot(scaled, p_prior)
        lq[here, :] += dot_t(dq, up_q[...])
        up_q_grad += t_dot(low_own[here, :rank], dq)
    own = dv_own[...].astype(BF16)
    prior = dv_prior[...].astype(BF16)
    lo[...] += dot(up_v[...], own)
    lp[...] += dot(up_v[...], prior)
    ups[0] = up_q_grad.astype(BF16)
    ups[1] = (dot(own, low_own[:, rank:]) + dot(prior, low_prior[:, rank:])).T.astype(BF16)

    @pl.when(head == heads - 1)
    def _():
        if ends:
            first = out.shape[1] - 4 * rank
            out[:, first : first + rank] = lq[...].astype(BF16)
            out[:, first + rank : first + 2 * rank] = lo[...].T.astype(BF16)
            out[:, first + 2 * rank : first + 3 * rank] = lp[...].T.astype(BF16)
            out[:, first + 3 * rank :] = jnp.zeros((rows, rank), BF16)
        else:
            low_out[0][...] = lq[...]
            low_out[1][...] = lo[...]
            low_out[2][...] = lp[...]


def attention(place, qg, k, k_prior, vl, vl_prior, up_q, up_v, lows, first, heads, ends):
    rows = qg.shape[0]
    total = k.shape[1] // HEAD
    rank = up_q.shape[0]
    begins = lows is None
    column = pl.BlockSpec((rows, HEAD), lambda h, place: (0, first + h))
    fixed = pl.BlockSpec((rows, HEAD), lambda h, place: (0, total))
    up = pl.BlockSpec((rank, HEAD), lambda h, place: (0, place[0] * total + first + h))
    shapes = ((rows, rank), (rank, rows), (rank, rows))
    whole = lambda shape: pl.BlockSpec(shape, lambda h, place: (0, 0))
    width = heads * HEAD
    out_width = width + 4 * rank if ends else width
    out_specs = [
        whole((rows, out_width)) if ends else pl.BlockSpec((rows, HEAD), lambda h, place: (0, h)),
        pl.BlockSpec((2, rank, HEAD), lambda h, place: (0, h, 0)),
    ]
    out_shape = [
        jax.ShapeDtypeStruct((rows, out_width), BF16),
        jax.ShapeDtypeStruct((2, heads * rank, HEAD), BF16),
    ]
    if not ends:
        out_specs += [whole(shape) for shape in shapes]
        out_shape += [jax.ShapeDtypeStruct(shape, F32) for shape in shapes]
    return pl.pallas_call(
        functools.partial(attention_kernel, begins, ends),
        grid_spec=pltpu.PrefetchScalarGridSpec(
            num_scalar_prefetch=1,
            grid=(heads,),
            in_specs=[
                pl.BlockSpec((rows, HEAD), lambda h, place: (0, h)),
                pl.BlockSpec((rows, HEAD), lambda h, place: (0, heads + h)),
                column,
                column,
                column,
                column,
                fixed,
                fixed,
                up,
                up,
            ]
            + ([] if begins else [whole(shape) for shape in shapes]),
            out_specs=out_specs,
            scratch_shapes=[pltpu.VMEM(shape, F32) for shape in shapes]
            + [pltpu.VMEM((HEAD, rows), F32)] * 2,
        ),
        out_shape=out_shape,
        compiler_params=pltpu.CompilerParams(vmem_limit_bytes=60 << 20),
        cost_estimate=pl.CostEstimate(
            flops=5 * 2 * heads * rows * 2 * rows * HEAD * 4,
            bytes_accessed=heads << 21,
            transcendentals=heads * rows * 2 * rows,
        ),
        name="attention",
    )(
        place, qg, qg, k, vl, k_prior, vl_prior, vl, vl_prior, up_q, up_v,
        *(() if begins else lows),
    )


def outer_kernel(lows, tokens, earlier, *rest):
    ups, out = rest[:-2], rest[-1]
    rows, columns = tokens.shape
    rank = lows.shape[1] // 4
    low = jnp.sum(lows[...].reshape(-1, rows, 4 * rank).astype(F32), axis=0).astype(BF16)
    grad_q = t_dot(low[:, :rank], tokens[...])
    grad_v = t_dot(low[:, rank : 2 * rank], tokens[...]) + t_dot(
        low[:, 2 * rank : 3 * rank], earlier[...]
    )
    for block in range(columns // HEAD):
        to = slice(block * rank, (block + 1) * rank)
        out[0, to, :] = grad_q[:, block * HEAD : (block + 1) * HEAD].astype(BF16)
        out[1, to, :] = grad_v[:, block * HEAD : (block + 1) * HEAD].astype(BF16)
    first = columns // HEAD * rank
    for up in ups:
        size = up.shape[1]
        out[:, first : first + size, :] = up[...]
        first += size


def outer(lows, tokens, earlier, ups, rank, settled):
    length = tokens.shape[1] // HEAD * rank + sum(up.shape[1] for up in ups)
    whole = lambda array: pl.BlockSpec(array.shape, lambda i: (0,) * array.ndim)
    at = lows.shape[1] // (4 * rank) - 1
    return pl.pallas_call(
        outer_kernel,
        grid=(1,),
        in_specs=[pl.BlockSpec((lows.shape[0], 4 * rank), lambda i: (0, at))]
        + [whole(array) for array in (tokens, earlier, *ups)]
        + [pl.BlockSpec(memory_space=pl.ANY)],
        out_specs=pl.BlockSpec((2, length, HEAD), lambda i: (0, 0, 0)),
        out_shape=jax.ShapeDtypeStruct((2, length, HEAD), BF16),
        compiler_params=pltpu.CompilerParams(vmem_limit_bytes=60 << 20),
        cost_estimate=pl.CostEstimate(flops=1 << 29, bytes_accessed=8 << 20, transcendentals=0),
        name="outer",
    )(lows, tokens, earlier, *ups, settled)


def unpack_kernel(both, down_q, down_v, up_q, up_v):
    rank, columns = down_q.shape
    first = columns // HEAD * rank
    for part, (down, up) in enumerate(((down_q, up_q), (down_v, up_v))):
        for block in range(columns // HEAD):
            down[:, block * HEAD : (block + 1) * HEAD] = both[
                part, block * rank : (block + 1) * rank, :
            ]
        for block in range(up.shape[1] // HEAD):
            up[:, block * HEAD : (block + 1) * HEAD] = both[
                part, first + block * rank : first + (block + 1) * rank, :
            ]


def unpack(both, rank, columns, width):
    return pl.pallas_call(
        unpack_kernel,
        out_shape=[jax.ShapeDtypeStruct((rank, columns), BF16)] * 2
        + [jax.ShapeDtypeStruct((rank, width), BF16)] * 2,
        compiler_params=pltpu.CompilerParams(vmem_limit_bytes=60 << 20),
        name="unpack",
    )(both)


def exchange(array, axis, groups=None):
    return lax.all_to_all(
        array, axis, split_axis=0, concat_axis=0, tiled=True, axis_index_groups=groups
    )


def summed(array, axis, size, groups=None):
    got = exchange(array, axis, groups)
    return jnp.sum(got.reshape(size, -1, array.shape[1]).astype(F32), axis=0).astype(BF16)


def gathered(array, axis, size, groups=None):
    copies = jnp.broadcast_to(array[None], (size,) + array.shape)
    return exchange(copies.reshape(-1, array.shape[1]), axis, groups)


def after(array, *others):
    return pl.pallas_call(
        lambda *refs: None,
        in_specs=[pl.BlockSpec(memory_space=pl.ANY)] * (1 + len(others)),
        out_specs=pl.BlockSpec(memory_space=pl.ANY),
        out_shape=jax.ShapeDtypeStruct(array.shape, array.dtype),
        input_output_aliases={0: 0},
        name="after",
    )(array, *others)


def per_device(tokens, query_base, key_base, value_base, out_grad, down_q, up_q, down_v, up_v):
    blocks = lax.axis_size("blk")
    parts = lax.axis_size("uly")
    rows, columns = tokens.shape
    rank = down_q.shape[1]
    width = columns // parts
    vl, qg_a, qg_b, copy = pack(
        tokens, query_base, value_base, out_grad, down_q.T, up_q, down_v.T, up_v, parts
    )
    forward = [(i, i + 1) for i in range(blocks - 1)]
    k = lax.all_to_all(key_base, "uly", split_axis=1, concat_axis=0, tiled=True)
    k_prior = lax.ppermute(k, "blk", forward)
    vl = exchange(after(vl, k), "uly")
    vl_prior = lax.ppermute(vl, "blk", forward)
    qg_a = exchange(after(qg_a, vl, k_prior), "uly")
    qg_b = exchange(after(qg_b, qg_a, vl_prior), "uly")
    earlier = lax.ppermute(after(copy, qg_a), "blk", forward)
    place = jnp.stack([lax.axis_index("uly"), lax.axis_index("blk")]).astype(jnp.int32)
    ready = (k, k_prior, vl, vl_prior, up_q, up_v)
    out, ups_a, *lows = attention(place, qg_a, *ready, None, 0, CALLS[0], False)
    piece = exchange(out, "uly")
    out, ups_b = attention(place, qg_b, *ready, lows, CALLS[0], CALLS[1], True)
    back = exchange(out, "uly")
    pieces = (piece, back)
    both = outer(back, tokens, earlier, (ups_a, ups_b), rank, piece)
    both = summed(both.reshape(-1, HEAD), "blk", 2, PAIR)
    length = columns // HEAD * rank
    down = summed(both[:length], "uly", parts)
    piece = length // parts // 8
    both = jnp.concatenate(
        [down.reshape(8, piece, HEAD), both[length:].reshape(8, -1, HEAD)], 1
    ).reshape(-1, HEAD)
    both = summed(both, "blk", 8, Z_RING)
    both = (both.astype(F32) + lax.ppermute(both, "blk", Y_PAIR).astype(F32)).astype(BF16)
    both = gathered(both, "blk", 8, Z_RING).reshape(8, -1, HEAD)
    down = gathered(both[:, :piece].reshape(-1, HEAD), "uly", parts)
    both = jnp.concatenate([down, both[:, piece:].reshape(-1, HEAD)], 0)
    both = gathered(both, "blk", 2, PAIR).reshape(2, -1, HEAD)
    down_q, down_v, up_q, up_v = unpack(both, rank, columns, width)
    attended = jnp.concatenate(
        [
            p.reshape(parts, rows, -1)[:, :, : heads * HEAD]
            for p, heads in zip(pieces, CALLS)
        ],
        2,
    )
    attended = attended.transpose(1, 0, 2).reshape(rows, columns)
    return (attended, down_q.T, up_q, down_v.T, up_v)


def solution(mesh):
    rows = P(("blk", "uly"), None)
    return jax.shard_map(
        per_device,
        mesh=mesh,
        in_specs=(rows,) * 5 + (P(),) * 4,
        out_specs=(rows, P(), P(None, "uly"), P(), P(None, "uly")),
        check_vma=False,
    )
```

```python
import functools

import jax
import jax.numpy as jnp
from jax import lax
from jax.experimental import pallas as pl
from jax.experimental.pallas import tpu as pltpu
from jax.sharding import PartitionSpec as P

HEAD = 128
TILE = 256
LOG2E = 1.4426950408889634
F32 = jnp.float32
BF16 = jnp.bfloat16
CALLS = (3, 2)

PAIR = [[2 * i, 2 * i + 1] for i in range(16)]
Z_RING = [[half * 16 + z * 2 + core for z in range(8)] for half in range(2) for core in range(2)]
Y_PAIR = [(i, i ^ 16) for i in range(32)]


def dot(left, right):
    return jnp.dot(left, right, preferred_element_type=F32)


def dot_t(left, right):
    return lax.dot_general(left, right, (((1,), (1,)), ((), ())), preferred_element_type=F32)


def t_dot(left, right):
    return lax.dot_general(left, right, (((0,), (0,)), ((), ())), preferred_element_type=F32)


def pack_kernel(
    tokens, query_base, value_base, out_grad, down_q, down_v, up_q, up_v, vl, *rest
):
    qgs, low = rest[:-1], rest[-1]
    rank = down_q.shape[0]
    width = value_base.shape[1]

    @pl.when(pl.program_id(0) == 0)
    def _():
        low[:, :rank] = dot_t(tokens[...], down_q[...]).astype(BF16)
        low[:, rank:] = dot_t(tokens[...], down_v[...]).astype(BF16)

    vl[:, : 2 * rank] = low[...]
    vl[:, 2 * rank :] = (value_base[...].astype(F32) + dot(low[:, rank:], up_v[...])).astype(
        BF16
    )
    query = (query_base[...].astype(F32) + dot(low[:, :rank], up_q[...])).astype(BF16)
    first = 0
    for qg, heads in zip(qgs, CALLS):
        part = heads * HEAD
        qg[:, :part] = query[:, first : first + part]
        qg[:, part:] = out_grad[:, first : first + part]
        first += part


def pack(tokens, query_base, value_base, out_grad, down_q, up_q, down_v, up_v, parts):
    rows, columns = tokens.shape
    rank = down_q.shape[0]
    width = columns // parts
    whole = lambda j: (0, 0)
    part = lambda j: (0, j)
    once = pl.Buffered(1)
    sizes = [width + 2 * rank] + [2 * heads * HEAD for heads in CALLS]
    return pl.pallas_call(
        pack_kernel,
        grid=(parts,),
        in_specs=[pl.BlockSpec((rows, columns), whole, pipeline_mode=once)]
        + [pl.BlockSpec((rows, width), part)] * 3
        + [pl.BlockSpec((rank, columns), whole, pipeline_mode=once)] * 2
        + [pl.BlockSpec((rank, width), part)] * 2,
        out_specs=[pl.BlockSpec((rows, size), lambda j: (j, 0)) for size in sizes],
        out_shape=[jax.ShapeDtypeStruct((parts * rows, size), BF16) for size in sizes],
        scratch_shapes=[pltpu.VMEM((rows, 2 * rank), BF16)],
        compiler_params=pltpu.CompilerParams(vmem_limit_bytes=60 << 20),
        cost_estimate=pl.CostEstimate(flops=1 << 29, bytes_accessed=14 << 20, transcendentals=0),
        name="pack",
    )(tokens, query_base, value_base, out_grad, down_q, down_v, up_q, up_v)


def attention_kernel(
    begins, ends, place, q, g, k_own, v_own, k_straight, v_straight, k_wrapped, v_wrapped,
    low_own, low_straight, low_wrapped, up_q, up_v, *rest,
):
    rest = list(rest)
    k_prior, v_prior = rest.pop(), rest.pop()
    k_prior[...] = k_straight[...] + k_wrapped[...]
    v_prior[...] = v_straight[...] + v_wrapped[...]
    low_in = None if begins else [rest.pop(0) for _ in range(3)]
    out, ups = rest.pop(0), rest.pop(0)
    low_out = None if ends else [rest.pop(0) for _ in range(3)]
    lq, lo, lp, dv_own, dv_prior = rest
    head = pl.program_id(0)
    heads = pl.num_programs(0)
    rows = q.shape[0]
    rank = up_q.shape[0]
    scale = HEAD ** (-0.5)
    factor = scale * LOG2E
    has_prior = place[1] > 0

    @pl.when(head == 0)
    def _():
        if begins:
            lq[...] = jnp.zeros_like(lq)
            lo[...] = jnp.zeros_like(lo)
            lp[...] = jnp.zeros_like(lp)
        else:
            lq[...] = low_in[0][...]
            lo[...] = low_in[1][...]
            lp[...] = low_in[2][...]

    def softmax(step):
        here = slice(step * TILE, (step + 1) * TILE)
        q_t = q[here, :]
        s_own = dot_t(q_t, k_own[...])
        s_prior = dot_t(q_t, k_prior[...])
        top_own = jnp.max(s_own, axis=1, keepdims=True)
        top_prior = jnp.max(s_prior, axis=1, keepdims=True)
        top = jnp.where(has_prior, jnp.maximum(top_own, top_prior), top_own) * factor
        top_p = jnp.where(has_prior, top, jnp.float32(1e38))
        p_own = jnp.exp2(s_own * factor - top)
        p_prior = jnp.exp2(s_prior * factor - top_p)
        total = jnp.sum(p_own, axis=1, keepdims=True) + jnp.sum(p_prior, axis=1, keepdims=True)
        return here, p_own.astype(BF16), p_prior.astype(BF16), 1.0 / total

    up_q_grad = jnp.zeros((rank, HEAD), F32)
    steps = rows // TILE
    following = softmax(0)
    for step in range(steps):
        here, p_own, p_prior, inverse = following
        if step + 1 < steps:
            following = softmax(step + 1)
        g_t = g[here, :]
        attended = ((dot(p_own, v_own[...]) + dot(p_prior, v_prior[...])) * inverse).astype(BF16)
        if ends:
            out[here, pl.ds(pl.multiple_of(head * HEAD, HEAD), HEAD)] = attended
        else:
            out[here, :] = attended
        delta = jnp.sum(g_t.astype(F32) * attended.astype(F32), axis=1, keepdims=True)
        ds_own = (p_own.astype(F32) * (dot_t(g_t, v_own[...]) - delta)).astype(BF16)
        ds_prior = (p_prior.astype(F32) * (dot_t(g_t, v_prior[...]) - delta)).astype(BF16)
        dq = ((dot(ds_own, k_own[...]) + dot(ds_prior, k_prior[...])) * (inverse * scale)).astype(
            BF16
        )
        scaled = (g_t.astype(F32) * inverse).astype(BF16)
        if step == 0:
            dv_own[...] = t_dot(scaled, p_own)
            dv_prior[...] = t_dot(scaled, p_prior)
        else:
            dv_own[...] += t_dot(scaled, p_own)
            dv_prior[...] += t_dot(scaled, p_prior)
        lq[here, :] += dot_t(dq, up_q[...])
        up_q_grad += t_dot(low_own[here, :rank], dq)
    own = dv_own[...].astype(BF16)
    prior = dv_prior[...].astype(BF16)
    lo[...] += dot(up_v[...], own)
    lp[...] += dot(up_v[...], prior)
    ups[0] = up_q_grad.astype(BF16)
    ups[1] = (dot(own, low_own[:, rank:]) + dot(prior, low_straight[:, rank:] + low_wrapped[:, rank:])).T.astype(BF16)

    @pl.when(head == heads - 1)
    def _():
        if ends:
            first = out.shape[1] - 4 * rank
            out[:, first : first + rank] = lq[...].astype(BF16)
            out[:, first + rank : first + 2 * rank] = lo[...].T.astype(BF16)
            out[:, first + 2 * rank : first + 3 * rank] = lp[...].T.astype(BF16)
            out[:, first + 3 * rank :] = jnp.zeros((rows, rank), BF16)
        else:
            low_out[0][...] = lq[...]
            low_out[1][...] = lo[...]
            low_out[2][...] = lp[...]


def attention(
    place, qg, k, k_prior, vl, vl_prior, low_wrap, up_q, up_v, wrap, lows, first, heads, ends
):
    rows = qg.shape[0]
    total = k.shape[1] // HEAD
    rank = up_q.shape[0]
    begins = lows is None
    column = lambda at: pl.BlockSpec((rows, HEAD), lambda h, place: (0, at + h))
    fixed = lambda at: pl.BlockSpec((rows, HEAD), lambda h, place: (0, at))
    up = pl.BlockSpec((rank, HEAD), lambda h, place: (0, place[0] * total + first + h))
    shapes = ((rows, rank), (rank, rows), (rank, rows))
    whole = lambda shape: pl.BlockSpec(shape, lambda h, place: (0, 0))
    width = heads * HEAD
    out_width = width + 4 * rank if ends else width
    out_specs = [
        whole((rows, out_width)) if ends else pl.BlockSpec((rows, HEAD), lambda h, place: (0, h)),
        pl.BlockSpec((2, rank, HEAD), lambda h, place: (0, h, 0)),
    ]
    out_shape = [
        jax.ShapeDtypeStruct((rows, out_width), BF16),
        jax.ShapeDtypeStruct((2, heads * rank, HEAD), BF16),
    ]
    if not ends:
        out_specs += [whole(shape) for shape in shapes]
        out_shape += [jax.ShapeDtypeStruct(shape, F32) for shape in shapes]
    return pl.pallas_call(
        functools.partial(attention_kernel, begins, ends),
        grid_spec=pltpu.PrefetchScalarGridSpec(
            num_scalar_prefetch=1,
            grid=(heads,),
            in_specs=[
                column(0),
                column(heads),
                column(first),
                column(first + 1),
                column(first),
                column(first + 1),
                column(0),
                column(wrap.shape[1] // HEAD - heads),
                fixed(0),
                fixed(0),
                fixed(CALLS[0]),
                up,
                up,
            ]
            + ([] if begins else [whole(shape) for shape in shapes]),
            out_specs=out_specs,
            scratch_shapes=[pltpu.VMEM(shape, F32) for shape in shapes]
            + [pltpu.VMEM((HEAD, rows), F32)] * 2
            + [pltpu.VMEM((rows, HEAD), BF16)] * 2,
        ),
        out_shape=out_shape,
        compiler_params=pltpu.CompilerParams(vmem_limit_bytes=60 << 20),
        cost_estimate=pl.CostEstimate(
            flops=5 * 2 * heads * rows * 2 * rows * HEAD * 4,
            bytes_accessed=heads << 21,
            transcendentals=heads * rows * 2 * rows,
        ),
        name="attention",
    )(
        place, qg, qg, k, vl, k_prior, vl_prior, wrap, wrap, vl, vl_prior, low_wrap, up_q, up_v,
        *(() if begins else lows),
    )


def outer_kernel(low, tokens, *rest):
    ups, out = rest[:-2], rest[-1]
    rank = low.shape[1] // 2
    columns = tokens.shape[1]
    grad_q = t_dot(low[:, :rank], tokens[...])
    grad_v = t_dot(low[:, rank:], tokens[...])
    for block in range(columns // HEAD):
        to = slice(block * rank, (block + 1) * rank)
        out[0, to, :] = grad_q[:, block * HEAD : (block + 1) * HEAD].astype(BF16)
        out[1, to, :] = grad_v[:, block * HEAD : (block + 1) * HEAD].astype(BF16)
    first = columns // HEAD * rank
    for up in ups:
        size = up.shape[1]
        out[:, first : first + size, :] = up[...]
        first += size


def outer(low, tokens, ups, settled):
    rank = low.shape[1] // 2
    length = tokens.shape[1] // HEAD * rank + sum(up.shape[1] for up in ups)
    whole = lambda array: pl.BlockSpec(array.shape, lambda i: (0,) * array.ndim)
    return pl.pallas_call(
        outer_kernel,
        grid=(1,),
        in_specs=[whole(array) for array in (low, tokens, *ups)]
        + [pl.BlockSpec(memory_space=pl.ANY)],
        out_specs=pl.BlockSpec((2, length, HEAD), lambda i: (0, 0, 0)),
        out_shape=jax.ShapeDtypeStruct((2, length, HEAD), BF16),
        compiler_params=pltpu.CompilerParams(vmem_limit_bytes=60 << 20),
        cost_estimate=pl.CostEstimate(flops=1 << 29, bytes_accessed=8 << 20, transcendentals=0),
        name="outer",
    )(low, tokens, *ups, settled)


def unpack_kernel(both, down_q, down_v, up_q, up_v):
    rank, columns = down_q.shape
    first = columns // HEAD * rank
    for part, (down, up) in enumerate(((down_q, up_q), (down_v, up_v))):
        for block in range(columns // HEAD):
            down[:, block * HEAD : (block + 1) * HEAD] = both[
                part, block * rank : (block + 1) * rank, :
            ]
        for block in range(up.shape[1] // HEAD):
            up[:, block * HEAD : (block + 1) * HEAD] = both[
                part, first + block * rank : first + (block + 1) * rank, :
            ]


def unpack(both, rank, columns, width):
    return pl.pallas_call(
        unpack_kernel,
        out_shape=[jax.ShapeDtypeStruct((rank, columns), BF16)] * 2
        + [jax.ShapeDtypeStruct((rank, width), BF16)] * 2,
        compiler_params=pltpu.CompilerParams(vmem_limit_bytes=60 << 20),
        name="unpack",
    )(both)


def exchange(array, axis, groups=None):
    return lax.all_to_all(
        array, axis, split_axis=0, concat_axis=0, tiled=True, axis_index_groups=groups
    )


def summed(array, axis, size, groups=None):
    got = exchange(array, axis, groups)
    return jnp.sum(got.reshape(size, -1, array.shape[1]).astype(F32), axis=0).astype(BF16)


def gathered(array, axis, size, groups=None):
    copies = jnp.broadcast_to(array[None], (size,) + array.shape)
    return exchange(copies.reshape(-1, array.shape[1]), axis, groups)


def after(array, *others):
    return pl.pallas_call(
        lambda *refs: None,
        in_specs=[pl.BlockSpec(memory_space=pl.ANY)] * (1 + len(others)),
        out_specs=pl.BlockSpec(memory_space=pl.ANY),
        out_shape=jax.ShapeDtypeStruct(array.shape, array.dtype),
        input_output_aliases={0: 0},
        name="after",
    )(array, *others)


def per_device(tokens, query_base, key_base, value_base, out_grad, down_q, up_q, down_v, up_v):
    blocks = lax.axis_size("blk")
    parts = lax.axis_size("uly")
    rows, columns = tokens.shape
    rank = down_q.shape[1]
    width = columns // parts
    vl, qg_a, qg_b = pack(
        tokens, query_base, value_base, out_grad, down_q.T, up_q, down_v.T, up_v, parts
    )
    crossing = blocks // 2 - 1
    forward = [(i, i + 1) for i in range(blocks - 1) if i != crossing]
    wrapped = [(crossing, crossing + 1)]
    k = lax.all_to_all(key_base, "uly", split_axis=1, concat_axis=0, tiled=True)
    k_prior = lax.ppermute(k, "blk", forward)
    vl = exchange(after(vl, k), "uly")
    vl_prior = lax.ppermute(vl, "blk", forward)
    qg_a = exchange(after(qg_a, vl, k_prior), "uly")
    split = CALLS[0] * HEAD
    wrap_a = jnp.concatenate([k[:, :split], vl[:, : split + 2 * rank]], 1)
    wrap_a = lax.ppermute(after(wrap_a, qg_a, vl_prior), "blk", wrapped)
    wrap_b = jnp.concatenate([k[:, split:], vl[:, split + 2 * rank :]], 1)
    wrap_b = lax.ppermute(after(wrap_b, wrap_a), "blk", wrapped)
    qg_b = exchange(after(qg_b, qg_a, vl_prior), "uly")
    place = jnp.stack([lax.axis_index("uly"), lax.axis_index("blk")]).astype(jnp.int32)
    ready = (k, k_prior, vl, vl_prior, wrap_a, up_q, up_v)
    out, ups_a, *lows = attention(place, qg_a, *ready, wrap_a, None, 0, CALLS[0], False)
    piece = exchange(out, "uly")
    out, ups_b = attention(place, qg_b, *ready, wrap_b, lows, CALLS[0], CALLS[1], True)
    back = exchange(after(out, piece), "uly")
    pieces = (piece, back)
    low = back.reshape(parts, rows, -1)[:, :, CALLS[1] * HEAD :].astype(F32)
    low = jnp.sum(low, axis=0)
    returned = lax.ppermute(
        low[:, 2 * rank : 3 * rank], "blk", [(i, i - 1) for i in range(1, blocks)]
    )
    low = jnp.concatenate([low[:, :rank], low[:, rank : 2 * rank] + returned], 1).astype(BF16)
    both = outer(low, tokens, (ups_a, ups_b), piece)
    both = summed(both.reshape(-1, HEAD), "blk", 2, PAIR)
    length = columns // HEAD * rank
    down = summed(both[:length], "uly", parts)
    piece = length // parts // 8
    both = jnp.concatenate(
        [down.reshape(8, piece, HEAD), both[length:].reshape(8, -1, HEAD)], 1
    ).reshape(-1, HEAD)
    both = summed(both, "blk", 8, Z_RING)
    both = (both.astype(F32) + lax.ppermute(both, "blk", Y_PAIR).astype(F32)).astype(BF16)
    both = gathered(both, "blk", 8, Z_RING).reshape(8, -1, HEAD)
    down = gathered(both[:, :piece].reshape(-1, HEAD), "uly", parts)
    both = jnp.concatenate([down, both[:, piece:].reshape(-1, HEAD)], 0)
    both = gathered(both, "blk", 2, PAIR).reshape(2, -1, HEAD)
    down_q, down_v, up_q, up_v = unpack(both, rank, columns, width)
    attended = jnp.concatenate(
        [
            p.reshape(parts, rows, -1)[:, :, : heads * HEAD]
            for p, heads in zip(pieces, CALLS)
        ],
        2,
    )
    attended = attended.transpose(1, 0, 2).reshape(rows, columns)
    return (attended, down_q.T, up_q, down_v.T, up_v)


def solution(mesh):
    rows = P(("blk", "uly"), None)
    return jax.shard_map(
        per_device,
        mesh=mesh,
        in_specs=(rows,) * 5 + (P(),) * 4,
        out_specs=(rows, P(), P(None, "uly"), P(), P(None, "uly")),
        check_vma=False,
    )
```

```python
import functools

import jax
import jax.numpy as jnp
from jax import lax
from jax.experimental import pallas as pl
from jax.experimental.pallas import tpu as pltpu
from jax.sharding import PartitionSpec as P

HEAD = 128
TILE = 256
LOG2E = 1.4426950408889634
F32 = jnp.float32
BF16 = jnp.bfloat16
CALLS = (2, 3)

PAIR = [[2 * i, 2 * i + 1] for i in range(16)]
Z_RING = [[half * 16 + z * 2 + core for z in range(8)] for half in range(2) for core in range(2)]
Y_PAIR = [(i, i ^ 16) for i in range(32)]


def dot(left, right):
    return jnp.dot(left, right, preferred_element_type=F32)


def dot_t(left, right):
    return lax.dot_general(left, right, (((1,), (1,)), ((), ())), preferred_element_type=F32)


def t_dot(left, right):
    return lax.dot_general(left, right, (((0,), (0,)), ((), ())), preferred_element_type=F32)


def pack_kernel(
    tokens, query_base, value_base, out_grad, down_q, down_v, up_q, up_v, vl, *rest
):
    qgs, copies, low = rest[:-3], rest[-3:-1], rest[-1]
    rank = down_q.shape[0]
    width = value_base.shape[1]

    @pl.when(pl.program_id(0) == 0)
    def _():
        low[:, :rank] = dot_t(tokens[...], down_q[...]).astype(BF16)
        low[:, rank:] = dot_t(tokens[...], down_v[...]).astype(BF16)
        for copy in copies:
            copy[...] = tokens[...]

    vl[:, : 2 * rank] = low[...]
    vl[:, 2 * rank :] = (value_base[...].astype(F32) + dot(low[:, rank:], up_v[...])).astype(
        BF16
    )
    query = (query_base[...].astype(F32) + dot(low[:, :rank], up_q[...])).astype(BF16)
    first = 0
    for qg, heads in zip(qgs, CALLS):
        part = heads * HEAD
        qg[:, :part] = query[:, first : first + part]
        qg[:, part:] = out_grad[:, first : first + part]
        first += part


def pack(tokens, query_base, value_base, out_grad, down_q, up_q, down_v, up_v, parts):
    rows, columns = tokens.shape
    rank = down_q.shape[0]
    width = columns // parts
    whole = lambda j: (0, 0)
    part = lambda j: (0, j)
    once = pl.Buffered(1)
    sizes = [width + 2 * rank] + [2 * heads * HEAD for heads in CALLS]
    return pl.pallas_call(
        pack_kernel,
        grid=(parts,),
        in_specs=[pl.BlockSpec((rows, columns), whole, pipeline_mode=once)]
        + [pl.BlockSpec((rows, width), part)] * 3
        + [pl.BlockSpec((rank, columns), whole, pipeline_mode=once)] * 2
        + [pl.BlockSpec((rank, width), part)] * 2,
        out_specs=[pl.BlockSpec((rows, size), lambda j: (j, 0)) for size in sizes]
        + [pl.BlockSpec((rows, columns), whole)] * 2,
        out_shape=[jax.ShapeDtypeStruct((parts * rows, size), BF16) for size in sizes]
        + [jax.ShapeDtypeStruct((rows, columns), BF16)] * 2,
        scratch_shapes=[pltpu.VMEM((rows, 2 * rank), BF16)],
        compiler_params=pltpu.CompilerParams(vmem_limit_bytes=60 << 20),
        cost_estimate=pl.CostEstimate(flops=1 << 29, bytes_accessed=14 << 20, transcendentals=0),
        name="pack",
    )(tokens, query_base, value_base, out_grad, down_q, down_v, up_q, up_v)


def attention_kernel(
    begins, ends, place, q, g, k_own, v_own, k_straight, v_straight, k_wrapped, v_wrapped,
    low_own, low_straight, low_wrapped, up_q, up_v, *rest,
):
    rest = list(rest)
    k_prior, v_prior = rest.pop(), rest.pop()
    k_prior[...] = k_straight[...] + k_wrapped[...]
    v_prior[...] = v_straight[...] + v_wrapped[...]
    low_in = None if begins else [rest.pop(0) for _ in range(3)]
    out, ups = rest.pop(0), rest.pop(0)
    low_out = None if ends else [rest.pop(0) for _ in range(3)]
    lq, lo, lp, dv_own, dv_prior = rest
    head = pl.program_id(0)
    heads = pl.num_programs(0)
    rows = q.shape[0]
    rank = up_q.shape[0]
    scale = HEAD ** (-0.5)
    factor = scale * LOG2E
    has_prior = place[1] > 0

    @pl.when(head == 0)
    def _():
        if begins:
            lq[...] = jnp.zeros_like(lq)
            lo[...] = jnp.zeros_like(lo)
            lp[...] = jnp.zeros_like(lp)
        else:
            lq[...] = low_in[0][...]
            lo[...] = low_in[1][...]
            lp[...] = low_in[2][...]

    def softmax(step):
        here = slice(step * TILE, (step + 1) * TILE)
        q_t = q[here, :]
        s_own = dot_t(q_t, k_own[...])
        s_prior = dot_t(q_t, k_prior[...])
        top_own = jnp.max(s_own, axis=1, keepdims=True)
        top_prior = jnp.max(s_prior, axis=1, keepdims=True)
        top = jnp.where(has_prior, jnp.maximum(top_own, top_prior), top_own) * factor
        top_p = jnp.where(has_prior, top, jnp.float32(1e38))
        p_own = jnp.exp2(s_own * factor - top)
        p_prior = jnp.exp2(s_prior * factor - top_p)
        total = jnp.sum(p_own, axis=1, keepdims=True) + jnp.sum(p_prior, axis=1, keepdims=True)
        return here, p_own.astype(BF16), p_prior.astype(BF16), 1.0 / total

    up_q_grad = jnp.zeros((rank, HEAD), F32)
    steps = rows // TILE
    following = softmax(0)
    for step in range(steps):
        here, p_own, p_prior, inverse = following
        if step + 1 < steps:
            following = softmax(step + 1)
        g_t = g[here, :]
        attended = ((dot(p_own, v_own[...]) + dot(p_prior, v_prior[...])) * inverse).astype(BF16)
        if ends:
            out[here, pl.ds(pl.multiple_of(head * HEAD, HEAD), HEAD)] = attended
        else:
            out[here, :] = attended
        delta = jnp.sum(g_t.astype(F32) * attended.astype(F32), axis=1, keepdims=True)
        ds_own = (p_own.astype(F32) * (dot_t(g_t, v_own[...]) - delta)).astype(BF16)
        ds_prior = (p_prior.astype(F32) * (dot_t(g_t, v_prior[...]) - delta)).astype(BF16)
        dq = ((dot(ds_own, k_own[...]) + dot(ds_prior, k_prior[...])) * (inverse * scale)).astype(
            BF16
        )
        scaled = (g_t.astype(F32) * inverse).astype(BF16)
        if step == 0:
            dv_own[...] = t_dot(scaled, p_own)
            dv_prior[...] = t_dot(scaled, p_prior)
        else:
            dv_own[...] += t_dot(scaled, p_own)
            dv_prior[...] += t_dot(scaled, p_prior)
        lq[here, :] += dot_t(dq, up_q[...])
        up_q_grad += t_dot(low_own[here, :rank], dq)
    own = dv_own[...].astype(BF16)
    prior = dv_prior[...].astype(BF16)
    lo[...] += dot(up_v[...], own)
    lp[...] += dot(up_v[...], prior)
    ups[0] = up_q_grad.astype(BF16)
    ups[1] = (dot(own, low_own[:, rank:]) + dot(prior, low_straight[:, rank:] + low_wrapped[:, rank:])).T.astype(BF16)

    @pl.when(head == heads - 1)
    def _():
        if ends:
            first = out.shape[1] - 4 * rank
            out[:, first : first + rank] = lq[...].astype(BF16)
            out[:, first + rank : first + 2 * rank] = lo[...].T.astype(BF16)
            out[:, first + 2 * rank : first + 3 * rank] = lp[...].T.astype(BF16)
            out[:, first + 3 * rank :] = jnp.zeros((rows, rank), BF16)
        else:
            low_out[0][...] = lq[...]
            low_out[1][...] = lo[...]
            low_out[2][...] = lp[...]


def attention(
    place, qg, k, k_prior, vl, vl_prior, low_wrap, up_q, up_v, wraps, lows, first, heads, ends
):
    rows = qg.shape[0]
    total = k.shape[1] // HEAD
    rank = up_q.shape[0]
    begins = lows is None
    column = lambda at: pl.BlockSpec((rows, HEAD), lambda h, place: (0, at + h))
    fixed = lambda at: pl.BlockSpec((rows, HEAD), lambda h, place: (0, at))
    up = pl.BlockSpec((rank, HEAD), lambda h, place: (0, place[0] * total + first + h))
    shapes = ((rows, rank), (rank, rows), (rank, rows))
    whole = lambda shape: pl.BlockSpec(shape, lambda h, place: (0, 0))
    width = heads * HEAD
    out_width = width + 4 * rank if ends else width
    out_specs = [
        whole((rows, out_width)) if ends else pl.BlockSpec((rows, HEAD), lambda h, place: (0, h)),
        pl.BlockSpec((2, rank, HEAD), lambda h, place: (0, h, 0)),
    ]
    out_shape = [
        jax.ShapeDtypeStruct((rows, out_width), BF16),
        jax.ShapeDtypeStruct((2, heads * rank, HEAD), BF16),
    ]
    if not ends:
        out_specs += [whole(shape) for shape in shapes]
        out_shape += [jax.ShapeDtypeStruct(shape, F32) for shape in shapes]
    return pl.pallas_call(
        functools.partial(attention_kernel, begins, ends),
        grid_spec=pltpu.PrefetchScalarGridSpec(
            num_scalar_prefetch=1,
            grid=(heads,),
            in_specs=[
                column(0),
                column(heads),
                column(first),
                column(first + 1),
                column(first),
                column(first + 1),
                column(0),
                column(0),
                fixed(0),
                fixed(0),
                fixed(0),
                up,
                up,
            ]
            + ([] if begins else [whole(shape) for shape in shapes]),
            out_specs=out_specs,
            scratch_shapes=[pltpu.VMEM(shape, F32) for shape in shapes]
            + [pltpu.VMEM((HEAD, rows), F32)] * 2
            + [pltpu.VMEM((rows, HEAD), BF16)] * 2,
        ),
        out_shape=out_shape,
        compiler_params=pltpu.CompilerParams(vmem_limit_bytes=60 << 20),
        cost_estimate=pl.CostEstimate(
            flops=5 * 2 * heads * rows * 2 * rows * HEAD * 4,
            bytes_accessed=heads << 21,
            transcendentals=heads * rows * 2 * rows,
        ),
        name="attention",
    )(
        place, qg, qg, k, vl, k_prior, vl_prior, *wraps, vl, vl_prior, low_wrap, up_q, up_v,
        *(() if begins else lows),
    )


def outer_kernel(lows, tokens, straight, wrapped, *rest):
    ups, out = rest[:-1], rest[-1]
    rows, columns = tokens.shape
    rank = lows.shape[1] // 4
    low = jnp.sum(lows[...].reshape(-1, rows, 4 * rank).astype(F32), axis=0).astype(BF16)
    grad_q = t_dot(low[:, :rank], tokens[...])
    grad_v = t_dot(low[:, rank : 2 * rank], tokens[...]) + t_dot(
        low[:, 2 * rank : 3 * rank], straight[...] + wrapped[...]
    )
    for block in range(columns // HEAD):
        to = slice(block * rank, (block + 1) * rank)
        out[0, to, :] = grad_q[:, block * HEAD : (block + 1) * HEAD].astype(BF16)
        out[1, to, :] = grad_v[:, block * HEAD : (block + 1) * HEAD].astype(BF16)
    first = columns // HEAD * rank
    for up in ups:
        size = up.shape[1]
        out[:, first : first + size, :] = up[...]
        first += size


def outer(lows, first, tokens, straight, wrapped, ups):
    columns = tokens.shape[1]
    rank = ups[0].shape[1] // CALLS[0]
    length = columns // HEAD * rank + sum(up.shape[1] for up in ups)
    whole = lambda array: pl.BlockSpec(array.shape, lambda i: (0,) * array.ndim)
    at = pl.BlockSpec(
        (pl.Element(lows.shape[0]), pl.Element(4 * rank)), lambda i: (0, first)
    )
    return pl.pallas_call(
        outer_kernel,
        grid=(1,),
        in_specs=[at] + [whole(array) for array in (tokens, straight, wrapped, *ups)],
        out_specs=pl.BlockSpec((2, length, HEAD), lambda i: (0, 0, 0)),
        out_shape=jax.ShapeDtypeStruct((2, length, HEAD), BF16),
        compiler_params=pltpu.CompilerParams(vmem_limit_bytes=60 << 20),
        cost_estimate=pl.CostEstimate(flops=1 << 29, bytes_accessed=8 << 20, transcendentals=0),
        name="outer",
    )(lows, tokens, straight, wrapped, *ups)


def unpack_kernel(both, down_q, down_v, up_q, up_v):
    rank, columns = down_q.shape
    first = columns // HEAD * rank
    for part, (down, up) in enumerate(((down_q, up_q), (down_v, up_v))):
        for block in range(columns // HEAD):
            down[:, block * HEAD : (block + 1) * HEAD] = both[
                part, block * rank : (block + 1) * rank, :
            ]
        for block in range(up.shape[1] // HEAD):
            up[:, block * HEAD : (block + 1) * HEAD] = both[
                part, first + block * rank : first + (block + 1) * rank, :
            ]


def unpack(both, rank, columns, width):
    return pl.pallas_call(
        unpack_kernel,
        out_shape=[jax.ShapeDtypeStruct((rank, columns), BF16)] * 2
        + [jax.ShapeDtypeStruct((rank, width), BF16)] * 2,
        compiler_params=pltpu.CompilerParams(vmem_limit_bytes=60 << 20),
        name="unpack",
    )(both)


def exchange(array, axis, groups=None):
    return lax.all_to_all(
        array, axis, split_axis=0, concat_axis=0, tiled=True, axis_index_groups=groups
    )


def summed(array, axis, size, groups=None):
    got = exchange(array, axis, groups)
    return jnp.sum(got.reshape(size, -1, array.shape[1]).astype(F32), axis=0).astype(BF16)


def gathered(array, axis, size, groups=None):
    copies = jnp.broadcast_to(array[None], (size,) + array.shape)
    return exchange(copies.reshape(-1, array.shape[1]), axis, groups)


def after(array, *others):
    return pl.pallas_call(
        lambda *refs: None,
        in_specs=[pl.BlockSpec(memory_space=pl.ANY)] * (1 + len(others)),
        out_specs=pl.BlockSpec(memory_space=pl.ANY),
        out_shape=jax.ShapeDtypeStruct(array.shape, array.dtype),
        input_output_aliases={0: 0},
        name="after",
    )(array, *others)


def per_device(tokens, query_base, key_base, value_base, out_grad, down_q, up_q, down_v, up_v):
    blocks = lax.axis_size("blk")
    parts = lax.axis_size("uly")
    rows, columns = tokens.shape
    rank = down_q.shape[1]
    width = columns // parts
    vl, qg_a, qg_b, copy_a, copy_b = pack(
        tokens, query_base, value_base, out_grad, down_q.T, up_q, down_v.T, up_v, parts
    )
    crossing = blocks // 2 - 1
    forward = [(i, i + 1) for i in range(blocks - 1) if i != crossing]
    wrapped = [(crossing, crossing + 1)]
    k = lax.all_to_all(key_base, "uly", split_axis=1, concat_axis=0, tiled=True)
    k_prior = lax.ppermute(k, "blk", forward)
    vl = exchange(after(vl, k), "uly")
    vl_prior = lax.ppermute(vl, "blk", forward)
    qg_a = exchange(after(qg_a, vl, k_prior), "uly")
    straight = lax.ppermute(after(copy_a, k_prior), "blk", forward)
    split = CALLS[0] * HEAD
    ready = (qg_a, vl_prior, straight)
    low_wrap, *wraps_a = [
        lax.ppermute(after(array, *ready), "blk", wrapped)
        for array in (
            vl[:, : 2 * rank],
            k[:, :split],
            vl[:, 2 * rank : 2 * rank + split],
        )
    ]
    wraps_b = [
        lax.ppermute(after(array, *wraps_a), "blk", wrapped)
        for array in (k[:, split:], vl[:, 2 * rank + split :])
    ]
    tokens_wrap = lax.ppermute(after(copy_b, *wraps_b), "blk", wrapped)
    qg_b = exchange(after(qg_b, qg_a, vl_prior), "uly")
    place = jnp.stack([lax.axis_index("uly"), lax.axis_index("blk")]).astype(jnp.int32)
    ready = (k, k_prior, vl, vl_prior, low_wrap, up_q, up_v)
    out, ups_a, *lows = attention(place, qg_a, *ready, wraps_a, None, 0, CALLS[0], False)
    piece = exchange(out, "uly")
    out, ups_b = attention(place, qg_b, *ready, wraps_b, lows, CALLS[0], CALLS[1], True)
    back = exchange(after(out, piece), "uly")
    pieces = (piece, back)
    both = outer(back, CALLS[1] * HEAD, tokens, straight, tokens_wrap, (ups_a, ups_b))
    both = summed(both.reshape(-1, HEAD), "blk", 2, PAIR)
    length = columns // HEAD * rank
    down = summed(both[:length], "uly", parts)
    piece = length // parts // 8
    both = jnp.concatenate(
        [down.reshape(8, piece, HEAD), both[length:].reshape(8, -1, HEAD)], 1
    ).reshape(-1, HEAD)
    both = summed(both, "blk", 8, Z_RING)
    both = (both.astype(F32) + lax.ppermute(both, "blk", Y_PAIR).astype(F32)).astype(BF16)
    both = gathered(both, "blk", 8, Z_RING).reshape(8, -1, HEAD)
    down = gathered(both[:, :piece].reshape(-1, HEAD), "uly", parts)
    both = jnp.concatenate([down, both[:, piece:].reshape(-1, HEAD)], 0)
    both = gathered(both, "blk", 2, PAIR).reshape(2, -1, HEAD)
    down_q, down_v, up_q, up_v = unpack(both, rank, columns, width)
    attended = jnp.concatenate(
        [
            p.reshape(parts, rows, -1)[:, :, : heads * HEAD]
            for p, heads in zip(pieces, CALLS)
        ],
        2,
    )
    attended = attended.transpose(1, 0, 2).reshape(rows, columns)
    return (attended, down_q.T, up_q, down_v.T, up_v)


def solution(mesh):
    rows = P(("blk", "uly"), None)
    return jax.shard_map(
        per_device,
        mesh=mesh,
        in_specs=(rows,) * 5 + (P(),) * 4,
        out_specs=(rows, P(), P(None, "uly"), P(), P(None, "uly")),
        check_vma=False,
    )
```

```python
import functools

import jax
import jax.numpy as jnp
from jax import lax
from jax.experimental import pallas as pl
from jax.experimental.pallas import tpu as pltpu
from jax.sharding import PartitionSpec as P

HEAD = 128
TILE = 256
LOG2E = 1.4426950408889634
F32 = jnp.float32
BF16 = jnp.bfloat16
CALLS = (2, 3)

PAIR = [[2 * i, 2 * i + 1] for i in range(16)]
Z_RING = [[half * 16 + z * 2 + core for z in range(8)] for half in range(2) for core in range(2)]
Y_PAIR = [(i, i ^ 16) for i in range(32)]


def dot(left, right):
    return jnp.dot(left, right, preferred_element_type=F32)


def dot_t(left, right):
    return lax.dot_general(left, right, (((1,), (1,)), ((), ())), preferred_element_type=F32)


def t_dot(left, right):
    return lax.dot_general(left, right, (((0,), (0,)), ((), ())), preferred_element_type=F32)


def pack_kernel(
    tokens, query_base, value_base, out_grad, down_q, down_v, up_q, up_v, vl, *rest
):
    qgs, copies, low = rest[:-3], rest[-3:-1], rest[-1]
    rank = down_q.shape[0]
    width = value_base.shape[1]

    @pl.when(pl.program_id(0) == 0)
    def _():
        low[:, :rank] = dot_t(tokens[...], down_q[...]).astype(BF16)
        low[:, rank:] = dot_t(tokens[...], down_v[...]).astype(BF16)
        for copy in copies:
            copy[...] = tokens[...]

    vl[:, : 2 * rank] = low[...]
    vl[:, 2 * rank :] = (value_base[...].astype(F32) + dot(low[:, rank:], up_v[...])).astype(
        BF16
    )
    query = (query_base[...].astype(F32) + dot(low[:, :rank], up_q[...])).astype(BF16)
    first = 0
    for qg, heads in zip(qgs, CALLS):
        part = heads * HEAD
        qg[:, :part] = query[:, first : first + part]
        qg[:, part:] = out_grad[:, first : first + part]
        first += part


def pack(tokens, query_base, value_base, out_grad, down_q, up_q, down_v, up_v, parts):
    rows, columns = tokens.shape
    rank = down_q.shape[0]
    width = columns // parts
    whole = lambda j: (0, 0)
    part = lambda j: (0, j)
    once = pl.Buffered(1)
    sizes = [width + 2 * rank] + [2 * heads * HEAD for heads in CALLS]
    return pl.pallas_call(
        pack_kernel,
        grid=(parts,),
        in_specs=[pl.BlockSpec((rows, columns), whole, pipeline_mode=once)]
        + [pl.BlockSpec((rows, width), part)] * 3
        + [pl.BlockSpec((rank, columns), whole, pipeline_mode=once)] * 2
        + [pl.BlockSpec((rank, width), part)] * 2,
        out_specs=[pl.BlockSpec((rows, size), lambda j: (j, 0)) for size in sizes]
        + [pl.BlockSpec((rows, columns), whole)] * 2,
        out_shape=[jax.ShapeDtypeStruct((parts * rows, size), BF16) for size in sizes]
        + [jax.ShapeDtypeStruct((rows, columns), BF16)] * 2,
        scratch_shapes=[pltpu.VMEM((rows, 2 * rank), BF16)],
        compiler_params=pltpu.CompilerParams(vmem_limit_bytes=60 << 20),
        cost_estimate=pl.CostEstimate(flops=1 << 29, bytes_accessed=14 << 20, transcendentals=0),
        name="pack",
    )(tokens, query_base, value_base, out_grad, down_q, down_v, up_q, up_v)


def cut_kernel(k, vl, low, k_a, v_a, k_b, v_b):
    rank2, split = low.shape[1], k_a.shape[1]
    low[...] = vl[:, :rank2]
    k_a[...] = k[:, :split]
    v_a[...] = vl[:, rank2 : rank2 + split]
    k_b[...] = k[:, split:]
    v_b[...] = vl[:, rank2 + split :]


def cut(k, vl):
    rows, columns = k.shape
    tile = rows // 4
    split = CALLS[0] * HEAD
    sizes = (vl.shape[1] - columns, split, split, columns - split, columns - split)
    block = lambda width: pl.BlockSpec((tile, width), lambda i: (i, 0))
    return pl.pallas_call(
        cut_kernel,
        grid=(rows // tile,),
        in_specs=[block(columns), block(vl.shape[1])],
        out_specs=[block(size) for size in sizes],
        out_shape=[jax.ShapeDtypeStruct((rows, size), BF16) for size in sizes],
        compiler_params=pltpu.CompilerParams(vmem_limit_bytes=60 << 20),
        cost_estimate=pl.CostEstimate(flops=0, bytes_accessed=6 << 20, transcendentals=0),
        name="cut",
    )(k, vl)


def attention_kernel(
    begins, ends, place, q, g, k_own, v_own, k_straight, v_straight, k_wrapped, v_wrapped,
    low_own, low_straight, low_wrapped, up_q, up_v, *rest,
):
    rest = list(rest)
    k_prior, v_prior = rest.pop(), rest.pop()
    k_prior[...] = k_straight[...] + k_wrapped[...]
    v_prior[...] = v_straight[...] + v_wrapped[...]
    low_in = None if begins else [rest.pop(0) for _ in range(3)]
    out, ups = rest.pop(0), rest.pop(0)
    low_out = None if ends else [rest.pop(0) for _ in range(3)]
    lq, lo, lp, dv_own, dv_prior = rest
    head = pl.program_id(0)
    heads = pl.num_programs(0)
    rows = q.shape[0]
    rank = up_q.shape[0]
    scale = HEAD ** (-0.5)
    factor = scale * LOG2E
    has_prior = place[1] > 0

    @pl.when(head == 0)
    def _():
        if begins:
            lq[...] = jnp.zeros_like(lq)
            lo[...] = jnp.zeros_like(lo)
            lp[...] = jnp.zeros_like(lp)
        else:
            lq[...] = low_in[0][...]
            lo[...] = low_in[1][...]
            lp[...] = low_in[2][...]

    def softmax(step):
        here = slice(step * TILE, (step + 1) * TILE)
        q_t = q[here, :]
        s_own = dot_t(q_t, k_own[...])
        s_prior = dot_t(q_t, k_prior[...])
        top_own = jnp.max(s_own, axis=1, keepdims=True)
        top_prior = jnp.max(s_prior, axis=1, keepdims=True)
        top = jnp.where(has_prior, jnp.maximum(top_own, top_prior), top_own) * factor
        top_p = jnp.where(has_prior, top, jnp.float32(1e38))
        p_own = jnp.exp2(s_own * factor - top)
        p_prior = jnp.exp2(s_prior * factor - top_p)
        total = jnp.sum(p_own, axis=1, keepdims=True) + jnp.sum(p_prior, axis=1, keepdims=True)
        return here, p_own.astype(BF16), p_prior.astype(BF16), 1.0 / total

    up_q_grad = jnp.zeros((rank, HEAD), F32)
    steps = rows // TILE
    following = softmax(0)
    for step in range(steps):
        here, p_own, p_prior, inverse = following
        if step + 1 < steps:
            following = softmax(step + 1)
        g_t = g[here, :]
        attended = ((dot(p_own, v_own[...]) + dot(p_prior, v_prior[...])) * inverse).astype(BF16)
        if ends:
            out[here, pl.ds(pl.multiple_of(head * HEAD, HEAD), HEAD)] = attended
        else:
            out[here, :] = attended
        delta = jnp.sum(g_t.astype(F32) * attended.astype(F32), axis=1, keepdims=True)
        ds_own = (p_own.astype(F32) * (dot_t(g_t, v_own[...]) - delta)).astype(BF16)
        ds_prior = (p_prior.astype(F32) * (dot_t(g_t, v_prior[...]) - delta)).astype(BF16)
        dq = ((dot(ds_own, k_own[...]) + dot(ds_prior, k_prior[...])) * (inverse * scale)).astype(
            BF16
        )
        scaled = (g_t.astype(F32) * inverse).astype(BF16)
        if step == 0:
            dv_own[...] = t_dot(scaled, p_own)
            dv_prior[...] = t_dot(scaled, p_prior)
        else:
            dv_own[...] += t_dot(scaled, p_own)
            dv_prior[...] += t_dot(scaled, p_prior)
        lq[here, :] += dot_t(dq, up_q[...])
        up_q_grad += t_dot(low_own[here, :rank], dq)
    own = dv_own[...].astype(BF16)
    prior = dv_prior[...].astype(BF16)
    lo[...] += dot(up_v[...], own)
    lp[...] += dot(up_v[...], prior)
    ups[0] = up_q_grad.astype(BF16)
    ups[1] = (dot(own, low_own[:, rank:]) + dot(prior, low_straight[:, rank:] + low_wrapped[:, rank:])).T.astype(BF16)

    @pl.when(head == heads - 1)
    def _():
        if ends:
            first = out.shape[1] - 4 * rank
            out[:, first : first + rank] = lq[...].astype(BF16)
            out[:, first + rank : first + 2 * rank] = lo[...].T.astype(BF16)
            out[:, first + 2 * rank : first + 3 * rank] = lp[...].T.astype(BF16)
            out[:, first + 3 * rank :] = jnp.zeros((rows, rank), BF16)
        else:
            low_out[0][...] = lq[...]
            low_out[1][...] = lo[...]
            low_out[2][...] = lp[...]


def attention(
    place, qg, k, k_prior, vl, vl_prior, low_wrap, up_q, up_v, wraps, lows, first, heads, ends
):
    rows = qg.shape[0]
    total = k.shape[1] // HEAD
    rank = up_q.shape[0]
    begins = lows is None
    column = lambda at: pl.BlockSpec((rows, HEAD), lambda h, place: (0, at + h))
    fixed = lambda at: pl.BlockSpec((rows, HEAD), lambda h, place: (0, at))
    up = pl.BlockSpec((rank, HEAD), lambda h, place: (0, place[0] * total + first + h))
    shapes = ((rows, rank), (rank, rows), (rank, rows))
    whole = lambda shape: pl.BlockSpec(shape, lambda h, place: (0, 0))
    width = heads * HEAD
    out_width = width + 4 * rank if ends else width
    out_specs = [
        whole((rows, out_width)) if ends else pl.BlockSpec((rows, HEAD), lambda h, place: (0, h)),
        pl.BlockSpec((2, rank, HEAD), lambda h, place: (0, h, 0)),
    ]
    out_shape = [
        jax.ShapeDtypeStruct((rows, out_width), BF16),
        jax.ShapeDtypeStruct((2, heads * rank, HEAD), BF16),
    ]
    if not ends:
        out_specs += [whole(shape) for shape in shapes]
        out_shape += [jax.ShapeDtypeStruct(shape, F32) for shape in shapes]
    return pl.pallas_call(
        functools.partial(attention_kernel, begins, ends),
        grid_spec=pltpu.PrefetchScalarGridSpec(
            num_scalar_prefetch=1,
            grid=(heads,),
            in_specs=[
                column(0),
                column(heads),
                column(first),
                column(first + 1),
                column(first),
                column(first + 1),
                column(0),
                column(0),
                fixed(0),
                fixed(0),
                fixed(0),
                up,
                up,
            ]
            + ([] if begins else [whole(shape) for shape in shapes]),
            out_specs=out_specs,
            scratch_shapes=[pltpu.VMEM(shape, F32) for shape in shapes]
            + [pltpu.VMEM((HEAD, rows), F32)] * 2
            + [pltpu.VMEM((rows, HEAD), BF16)] * 2,
        ),
        out_shape=out_shape,
        compiler_params=pltpu.CompilerParams(vmem_limit_bytes=60 << 20),
        cost_estimate=pl.CostEstimate(
            flops=5 * 2 * heads * rows * 2 * rows * HEAD * 4,
            bytes_accessed=heads << 21,
            transcendentals=heads * rows * 2 * rows,
        ),
        name="attention",
    )(
        place, qg, qg, k, vl, k_prior, vl_prior, *wraps, vl, vl_prior, low_wrap, up_q, up_v,
        *(() if begins else lows),
    )


def outer_kernel(lows, tokens, straight, wrapped, *rest):
    ups, out = rest[:-1], rest[-1]
    rows, columns = tokens.shape
    rank = lows.shape[1] // 4
    low = jnp.sum(lows[...].reshape(-1, rows, 4 * rank).astype(F32), axis=0).astype(BF16)
    grad_q = t_dot(low[:, :rank], tokens[...])
    grad_v = t_dot(low[:, rank : 2 * rank], tokens[...]) + t_dot(
        low[:, 2 * rank : 3 * rank], straight[...] + wrapped[...]
    )
    for block in range(columns // HEAD):
        to = slice(block * rank, (block + 1) * rank)
        out[0, to, :] = grad_q[:, block * HEAD : (block + 1) * HEAD].astype(BF16)
        out[1, to, :] = grad_v[:, block * HEAD : (block + 1) * HEAD].astype(BF16)
    first = columns // HEAD * rank
    for up in ups:
        size = up.shape[1]
        out[:, first : first + size, :] = up[...]
        first += size


def outer(lows, first, tokens, straight, wrapped, ups):
    columns = tokens.shape[1]
    rank = ups[0].shape[1] // CALLS[0]
    length = columns // HEAD * rank + sum(up.shape[1] for up in ups)
    whole = lambda array: pl.BlockSpec(array.shape, lambda i: (0,) * array.ndim)
    at = pl.BlockSpec(
        (pl.Element(lows.shape[0]), pl.Element(4 * rank)), lambda i: (0, first)
    )
    return pl.pallas_call(
        outer_kernel,
        grid=(1,),
        in_specs=[at] + [whole(array) for array in (tokens, straight, wrapped, *ups)],
        out_specs=pl.BlockSpec((2, length, HEAD), lambda i: (0, 0, 0)),
        out_shape=jax.ShapeDtypeStruct((2, length, HEAD), BF16),
        compiler_params=pltpu.CompilerParams(vmem_limit_bytes=60 << 20),
        cost_estimate=pl.CostEstimate(flops=1 << 29, bytes_accessed=8 << 20, transcendentals=0),
        name="outer",
    )(lows, tokens, straight, wrapped, *ups)


def unpack_kernel(both, down_q, down_v, up_q, up_v):
    rank, columns = down_q.shape
    first = columns // HEAD * rank
    for part, (down, up) in enumerate(((down_q, up_q), (down_v, up_v))):
        for block in range(columns // HEAD):
            down[:, block * HEAD : (block + 1) * HEAD] = both[
                part, block * rank : (block + 1) * rank, :
            ]
        for block in range(up.shape[1] // HEAD):
            up[:, block * HEAD : (block + 1) * HEAD] = both[
                part, first + block * rank : first + (block + 1) * rank, :
            ]


def unpack(both, rank, columns, width):
    return pl.pallas_call(
        unpack_kernel,
        out_shape=[jax.ShapeDtypeStruct((rank, columns), BF16)] * 2
        + [jax.ShapeDtypeStruct((rank, width), BF16)] * 2,
        compiler_params=pltpu.CompilerParams(vmem_limit_bytes=60 << 20),
        name="unpack",
    )(both)


def exchange(array, axis, groups=None):
    return lax.all_to_all(
        array, axis, split_axis=0, concat_axis=0, tiled=True, axis_index_groups=groups
    )


def summed(array, axis, size, groups=None):
    got = exchange(array, axis, groups)
    return jnp.sum(got.reshape(size, -1, array.shape[1]).astype(F32), axis=0).astype(BF16)


def gathered(array, axis, size, groups=None):
    copies = jnp.broadcast_to(array[None], (size,) + array.shape)
    return exchange(copies.reshape(-1, array.shape[1]), axis, groups)


def after(array, *others):
    return pl.pallas_call(
        lambda *refs: None,
        in_specs=[pl.BlockSpec(memory_space=pl.ANY)] * (1 + len(others)),
        out_specs=pl.BlockSpec(memory_space=pl.ANY),
        out_shape=jax.ShapeDtypeStruct(array.shape, array.dtype),
        input_output_aliases={0: 0},
        name="after",
    )(array, *others)


def per_device(tokens, query_base, key_base, value_base, out_grad, down_q, up_q, down_v, up_v):
    blocks = lax.axis_size("blk")
    parts = lax.axis_size("uly")
    rows, columns = tokens.shape
    rank = down_q.shape[1]
    width = columns // parts
    vl, qg_a, qg_b, copy_a, copy_b = pack(
        tokens, query_base, value_base, out_grad, down_q.T, up_q, down_v.T, up_v, parts
    )
    crossing = blocks // 2 - 1
    forward = [(i, i + 1) for i in range(blocks - 1) if i != crossing]
    wrapped = [(crossing, crossing + 1)]
    k = lax.all_to_all(key_base, "uly", split_axis=1, concat_axis=0, tiled=True)
    k_prior = lax.ppermute(k, "blk", forward)
    vl = exchange(after(vl, k), "uly")
    vl_prior = lax.ppermute(vl, "blk", forward)
    qg_a = exchange(after(qg_a, vl, k_prior), "uly")
    straight = lax.ppermute(after(copy_a, k_prior), "blk", forward)
    pieces = cut(k, vl)
    low_wrap, *wraps_a = [
        lax.ppermute(after(array, qg_a, vl_prior), "blk", wrapped) for array in pieces[:3]
    ]
    wraps_b = [
        lax.ppermute(after(array, wraps_a[1]), "blk", wrapped) for array in pieces[3:]
    ]
    tokens_wrap = lax.ppermute(after(copy_b, *wraps_b, straight), "blk", wrapped)
    qg_b = exchange(after(qg_b, qg_a, vl_prior), "uly")
    place = jnp.stack([lax.axis_index("uly"), lax.axis_index("blk")]).astype(jnp.int32)
    ready = (k, k_prior, vl, vl_prior, low_wrap, up_q, up_v)
    out, ups_a, *lows = attention(place, qg_a, *ready, wraps_a, None, 0, CALLS[0], False)
    piece = exchange(out, "uly")
    out, ups_b = attention(place, qg_b, *ready, wraps_b, lows, CALLS[0], CALLS[1], True)
    back = exchange(after(out, piece), "uly")
    pieces = (piece, back)
    both = outer(back, CALLS[1] * HEAD, tokens, straight, tokens_wrap, (ups_a, ups_b))
    both = summed(both.reshape(-1, HEAD), "blk", 2, PAIR)
    length = columns // HEAD * rank
    down = summed(both[:length], "uly", parts)
    piece = length // parts // 8
    both = jnp.concatenate(
        [down.reshape(8, piece, HEAD), both[length:].reshape(8, -1, HEAD)], 1
    ).reshape(-1, HEAD)
    both = summed(both, "blk", 8, Z_RING)
    both = (both.astype(F32) + lax.ppermute(both, "blk", Y_PAIR).astype(F32)).astype(BF16)
    both = gathered(both, "blk", 8, Z_RING).reshape(8, -1, HEAD)
    down = gathered(both[:, :piece].reshape(-1, HEAD), "uly", parts)
    both = jnp.concatenate([down, both[:, piece:].reshape(-1, HEAD)], 0)
    both = gathered(both, "blk", 2, PAIR).reshape(2, -1, HEAD)
    down_q, down_v, up_q, up_v = unpack(both, rank, columns, width)
    attended = jnp.concatenate(
        [
            p.reshape(parts, rows, -1)[:, :, : heads * HEAD]
            for p, heads in zip(pieces, CALLS)
        ],
        2,
    )
    attended = attended.transpose(1, 0, 2).reshape(rows, columns)
    return (attended, down_q.T, up_q, down_v.T, up_v)


def solution(mesh):
    rows = P(("blk", "uly"), None)
    return jax.shard_map(
        per_device,
        mesh=mesh,
        in_specs=(rows,) * 5 + (P(),) * 4,
        out_specs=(rows, P(), P(None, "uly"), P(), P(None, "uly")),
        check_vma=False,
    )
```
